32 devices in a mesh: rows: 8 (over y, x, core), cols: 4 (over z).
Axes of the slice: x: 2, y: 2, z: 4, core: 2. Of those that a mesh axis runs over, the one named last changes fastest.
Arguments:
- matrix: float32 [4096, 4096], P('rows', 'cols'), may hold values from -24 to 24
- gap_table: float32 [2, 2048, 256], P(None, 'rows'), may hold values from 8 to 32
- orders: int32 [2, 8, 2], replicated, may hold values from 0 to 1, each once within a row
Outputs:
- result: float32 [4096, 4096], P('rows', 'cols')
The draws below stay inside these ranges and needn't reach their ends.
Inputs may be any that keep to these rules, and one draw needn't show every extreme that they name: `orders`: each pair's two entries are 0 and 1 in some order.
All inputs are finite; a program needn't handle non-finite values.
Results may differ from the reference program's by a relative error of at most 0.00029.
Values sent between devices are 32-bit elements; how exact they have to be, the bound alone decides.
No kernel may reach another device: no remote copies, remote signals or barrier semaphores. Data moves between devices by JAX's collectives and lax.ppermute only.
A program may use at most 64 MiB of HBM per device.

```python
import math
import jax
import jax.numpy as jnp
from jax import lax

BLK = 256
STEPS = 2
PAIRS = 8
ORDER = 4096


def draw_matrix(key, part):
    samples = jax.random.normal(key, (ORDER, ORDER), jnp.float32)
    symmetric = jnp.clip((samples + samples.T) * 0.7071067811865476, -6.0, 6.0)
    return symmetric


def block_levels(stream_key, shape, pieces, low, largest):
    gain, own = 1.0, jax.random.fold_in(stream_key, 6)
    for position, parts in pieces:
        heights = jnp.exp(jax.random.uniform(jax.random.fold_in(own, position), (parts,), jnp.float32, low / len(pieces), largest / len(pieces)))
        gain = gain * jnp.repeat(heights, shape[position] // parts).reshape([-1 if axis == position else 1 for axis in range(len(shape))])
    return gain


def setup_inputs(seed: int = 0) -> dict:
    key_list = jax.random.split(jax.random.key(seed), 4)
    matrix = draw_matrix(jax.random.fold_in(key_list[3], 71), 0)
    gap_table = jnp.clip(jnp.exp(math.log(32.0) - 1.3862944 * jax.random.uniform(key_list[1], (STEPS, PAIRS * BLK, BLK), jnp.float32) ** block_levels(key_list[1], (STEPS, PAIRS * BLK, BLK), ((1, 8),), -0.2, 0.2)), 8.0, 32.0)
    orders = jax.vmap(lambda own: jax.random.permutation(own, 2))(jax.random.split(key_list[2], STEPS * PAIRS)).reshape((STEPS, PAIRS, 2)).astype(jnp.int32)
    return {"matrix": matrix, "gap_table": gap_table, "orders": orders}


highest = lax.Precision.HIGHEST

def rotation(generator):
    block_width = generator.shape[0]
    identity = jnp.eye(block_width, dtype=generator.dtype)
    shifted = identity + jnp.dot(generator.T, generator, precision=highest)
    factor = jnp.linalg.cholesky(shifted)
    inverse_root = lax.linalg.triangular_solve(factor, identity, left_side=True, lower=True)
    weight = jnp.dot(inverse_root.T, inverse_root, precision=highest)
    product = jnp.dot(generator, weight, precision=highest)
    upper_half = jnp.concatenate([identity - 2.0 * jnp.dot(product, generator.T, precision=highest), 2.0 * product], 1)
    lower_half = jnp.concatenate([-2.0 * product.T, 2.0 * weight - identity], 1)
    return jnp.concatenate([upper_half, lower_half], 0)

def reference(matrix, gap_table, orders):
    block_width = gap_table.shape[2]
    pair_count = gap_table.shape[1] // block_width
    pair_width = 2 * block_width
    matrix_order = matrix.shape[0]
    pair_ids = jnp.arange(pair_count).astype(jnp.int32)
    for sweep_step in range(orders.shape[0]):
        blocks = matrix.reshape(pair_count, pair_width, pair_count, pair_width)
        diagonal = blocks[pair_ids, :, pair_ids, :]
        coupling = diagonal[:, :block_width, block_width:]
        generators = coupling / (2.0 * gap_table[sweep_step].reshape(pair_count, block_width, block_width))
        rotations = jax.vmap(rotation)(generators)
        row_view = matrix.reshape(pair_count, pair_width, matrix_order)
        row_view = jnp.einsum('kba,kbn->kan', rotations, row_view, precision=highest)
        col_view = row_view.reshape(matrix_order, pair_count, pair_width)
        col_view = jnp.einsum('nkb,kbc->nkc', col_view, rotations, precision=highest)
        matrix = col_view.reshape(matrix_order, matrix_order)
        step_orders = orders[sweep_step]
        previous = jnp.roll(pair_ids, 1)
        staying = 2 * pair_ids + step_orders[:, 0]
        arriving = 2 * previous + step_orders[previous, 1]
        block_order = jnp.stack([staying, arriving], 1).reshape(-1).astype(jnp.int32)
        element_order = (block_order[:, None] * block_width + jnp.arange(block_width).astype(jnp.int32)[None, :]).reshape(-1).astype(jnp.int32)
        matrix = jnp.take(matrix, element_order, axis=0)
        matrix = jnp.take(matrix, element_order, axis=1)
    return matrix
```

```python
import functools
import jax
import jax.numpy as jnp
from jax import lax
from jax.experimental import pallas as pl
from jax.experimental.pallas import tpu as pltpu
from jax.sharding import PartitionSpec as P


F32 = jnp.float32
BF16 = jnp.bfloat16
HIGHEST = lax.Precision.HIGHEST
EASY_NORM = 12.0

ANY = pl.BlockSpec(memory_space=pl.ANY)
VMEM = pl.BlockSpec(memory_space=pltpu.VMEM)
SMEM = pl.BlockSpec(memory_space=pltpu.SMEM)


def split(value):
    high = value.astype(BF16)
    low = (value - high.astype(F32)).astype(BF16)
    return high, low


def coarse_dot(left, right):
    return jnp.dot(left.astype(BF16), right.astype(BF16), preferred_element_type=F32)


def fine_dot(left, right):
    (left_high, left_low), (right_high, right_low) = left, right
    dot = functools.partial(jnp.dot, preferred_element_type=F32)
    return dot(left_high, right_high) + (dot(left_high, right_low) + dot(left_low, right_high))


def full_dot(left, right):
    return jnp.dot(left, right, precision=HIGHEST, preferred_element_type=F32)


def factors(generator, weight):
    return split(generator), split(generator.T), split(weight)


def turn_rows(first, second, parts):
    plain, flipped, weight = parts
    mixed = fine_dot(flipped, split(first)) + second
    image = 2.0 * fine_dot(weight, split(mixed))
    return first - fine_dot(plain, split(image)), image - second


def turn_columns(first, second, parts):
    plain, flipped, weight = parts
    mixed = fine_dot(split(first), plain) + second
    image = 2.0 * fine_dot(split(mixed), weight)
    return first - fine_dot(split(image), flipped), image - second


def eye(width):
    shape = (width, width)
    return (lax.broadcasted_iota(jnp.int32, shape, 0) == lax.broadcasted_iota(jnp.int32, shape, 1)).astype(F32)


def invert(generators, weights):
    count, width = generators.shape[0], generators.shape[1]
    identity = eye(width)
    every = range(count)
    flipped = [generators[q].T for q in every]
    shifted = [identity + fine_dot(split(flipped[q]), split(generators[q])) for q in every]
    bounds = [jnp.max(jnp.sum(jnp.abs(m), axis=0, keepdims=True), axis=1, keepdims=True) for m in shifted]
    worst = bounds[0]
    for bound in bounds[1:]:
        worst = jnp.maximum(worst, bound)
    norm = jnp.max(worst)

    @pl.when(norm <= EASY_NORM)
    def _():
        scale = [8.0 / (2.0 * (b + 1.0) * (b + 1.0) - (b - 1.0) * (b - 1.0)) for b in bounds]
        linear = [scale[q] * (bounds[q] + 1.0) for q in every]
        guess = [linear[q] * identity - scale[q] * shifted[q] for q in every]
        square = [coarse_dot(m, m) for m in shifted]
        rest = [identity - linear[q] * shifted[q] + scale[q] * square[q] for q in every]
        for last in (False, False, True):
            step = [coarse_dot(guess[q], rest[q]) for q in every]
            if not last:
                rest = [coarse_dot(m, m) for m in rest]
            guess = [guess[q] + step[q] for q in every]
        for _ in range(2):
            rest = [identity - fine_dot(split(shifted[q]), split(guess[q])) for q in every]
            guess = [guess[q] + coarse_dot(guess[q], rest[q]) for q in every]
        for q in every:
            weights[q] = guess[q]

    @pl.when(norm > EASY_NORM)
    def _():
        rounds = jnp.int32(10)
        for power in range(30):
            rounds += (norm > EASY_NORM * 2.0**power).astype(jnp.int32)

        def solve(q, carry):
            plain = generators[q]
            system = identity + full_dot(plain.T, plain)
            weights[q] = (2.0 / (1.0 + norm)) * identity

            def improve(_, carry):
                guess = weights[q]
                weights[q] = guess + full_dot(guess, identity - full_dot(system, guess))
                return carry

            return lax.fori_loop(0, rounds, improve, carry)

        lax.fori_loop(0, count, solve, 0)


def places(shape):
    rows, cols = shape
    band_pairs = rows // cols
    row, col = lax.axis_index("rows"), lax.axis_index("cols")
    return row, col, lax.div(row, band_pairs), lax.rem(row, band_pairs)


def first_generators_kernel(shape, matrix, gap_table, out, coupling, gap, sems):
    width = out.shape[0]
    row, col, group, lane = places(shape)
    anchor = pl.multiple_of(lane * (2 * width) + width, width)
    copies = (
        pltpu.make_async_copy(matrix.at[pl.ds(0, width), pl.ds(anchor, width)], coupling, sems.at[0]),
        pltpu.make_async_copy(gap_table.at[0], gap, sems.at[1]),
    )
    for copy in copies:
        copy.start()
    for copy in copies:
        copy.wait()
    out[...] = jnp.where(group == col, coupling[...] / (2.0 * gap[...]), 0.0)


def gather_generators(shape, row_parts, band_parts, generators):
    band_pairs = shape[0] // shape[1]
    lane = places(shape)[3]
    generators[0] = row_parts[0][...] + row_parts[1][...]
    for shift, part in enumerate(band_parts):
        generators[1 + lax.rem(lane - shift + band_pairs, band_pairs)] = part[...]


def weights_kernel(shape, *refs):
    band_pairs = shape[0] // shape[1]
    row_parts, band_parts, (generators, weights) = refs[:2], refs[2 : 2 + band_pairs], refs[2 + band_pairs :]
    gather_generators(shape, row_parts, band_parts, generators)
    invert(generators, weights)


def weights_and_next_kernel(shape, step, *refs):
    band_pairs = shape[0] // shape[1]
    orders, matrix, gap_table, row_parts = refs[0], refs[1], refs[2], refs[3:5]
    band_parts, (generators, weights, out, block, gap, sems) = refs[5 : 5 + band_pairs], refs[5 + band_pairs :]
    width = out.shape[0]
    row, col, group, lane = places(shape)
    before = lax.rem(row - 1 + shape[0], shape[0])
    pair = lax.rem(before, band_pairs)
    start = pl.multiple_of(pair * (2 * width), 2 * width)
    copies = (
        pltpu.make_async_copy(matrix.at[:, pl.ds(start, 2 * width)], block, sems.at[0]),
        pltpu.make_async_copy(gap_table.at[step + 1], gap, sems.at[1]),
    )
    for copy in copies:
        copy.start()
    gather_generators(shape, row_parts, band_parts, generators)
    invert(generators, weights)
    for copy in copies:
        copy.wait()
    top, bottom = turn_rows(block[:width], block[width:], factors(generators[0], weights[0]))
    stay = jnp.where(orders[step, row, 0] == 0, top, bottom)
    left, right = turn_columns(stay[:, :width], stay[:, width:], factors(generators[1 + pair], weights[1 + pair]))
    coupling = jnp.where(orders[step, before, 1] == 0, left, right)
    here = lax.div(before, band_pairs) == col
    out[...] = jnp.where(here, coupling / (2.0 * gap[...]), 0.0)


def rotate_kernel(shape, step, sources, *refs):
    count = 1 + max(source[0] for source in sources)
    orders, inputs, generators, weights = refs[0], refs[1 : 1 + count], refs[1 + count], refs[2 + count]
    stay_out, row_out, col_out, corner_out, block, sems = refs[3 + count :]
    width = generators.shape[1]
    band_pairs = generators.shape[0] - 1
    row, col, group, lane = places(shape)
    copies = []
    for index, (which, source_row, source_col, rows, cols, to_row, to_col) in enumerate(sources):
        copies.append(
            pltpu.make_async_copy(
                inputs[which].at[pl.ds(source_row, rows), pl.ds(source_col, cols)],
                block.at[pl.ds(to_row, rows), pl.ds(to_col, cols)],
                sems.at[index],
            )
        )
    for copy in copies:
        copy.start()
    own = factors(generators[0], weights[0])
    for copy in copies:
        copy.wait()
    keep_rows = orders[step, row, 0] == 0
    for pair in range(band_pairs):
        cols = pl.ds(pair * 2 * width, 2 * width)
        top, bottom = turn_rows(block[:width, cols], block[width:, cols], own)
        parts = factors(generators[1 + pair], weights[1 + pair])
        keep_cols = orders[step, col * band_pairs + pair, 0] == 0
        for leaves in (True, False):
            picked = jnp.where(keep_rows != leaves, top, bottom)
            left, right = turn_columns(picked[:, :width], picked[:, width:], parts)
            stay, away = jnp.where(keep_cols, left, right), jnp.where(keep_cols, right, left)
            if leaves:
                row_out[:, pl.ds(max(2 * pair - 1, 0) * width, width)] = stay
                if pair < band_pairs - 1:
                    row_out[:, pl.ds((2 * pair + 2) * width, width)] = away
                else:
                    corner_out[...] = away
            else:
                stay_out[:width, pl.ds(2 * pair * width, width)] = stay
                if pair < band_pairs - 1:
                    stay_out[:width, pl.ds((2 * pair + 3) * width, width)] = away
                else:
                    col_out[...] = away


def fill_kernel(width, partial, row_in, col_in, corner_in, out, sems):
    del partial
    wide = out.shape[1]
    copies = (
        pltpu.make_async_copy(row_in.at[:, pl.ds(0, width)], out.at[pl.ds(width, width), pl.ds(0, width)], sems.at[0]),
        pltpu.make_async_copy(
            row_in.at[:, pl.ds(width, wide - 2 * width)],
            out.at[pl.ds(width, width), pl.ds(2 * width, wide - 2 * width)],
            sems.at[1],
        ),
        pltpu.make_async_copy(col_in, out.at[pl.ds(0, width), pl.ds(width, width)], sems.at[2]),
        pltpu.make_async_copy(corner_in, out.at[pl.ds(width, width), pl.ds(width, width)], sems.at[3]),
    )
    for copy in copies:
        copy.start()
    for copy in copies:
        copy.wait()


def send(value, pairs):
    return lax.ppermute(value, ("rows", "cols"), pairs)


def bits_below(count):
    return [1 << bit for bit in range((count - 1).bit_length())]


def first_row_rounds(shape):
    rows, cols = shape
    band_pairs = rows // cols
    held, rounds = [0], []
    for bit in reversed(bits_below(cols)):
        source = lambda row: row // band_pairs
        rounds.append([(row * cols + (source(row) ^ d), row * cols + (source(row) ^ d ^ bit)) for row in range(rows) for d in held])
        held = held + [d ^ bit for d in held]
    return rounds


def later_row_rounds(shape):
    rows, cols = shape
    band_pairs = rows // cols
    held, rounds = [0], []
    for bit in bits_below(cols):
        source = lambda row: (row - 1) % rows // band_pairs
        rounds.append(
            [(row * cols + (source(row) + d) % cols, row * cols + (source(row) + d + bit) % cols) for row in range(rows) for d in held]
        )
        held = held + [d + bit for d in held]
    return rounds


def band_rounds(shape):
    rows, cols = shape
    band_pairs = rows // cols
    held, rounds = [0], []
    for bit in reversed(bits_below(cols)):
        rounds.append(
            [
                (((col ^ d) * band_pairs + lane) * cols + col, ((col ^ d ^ bit) * band_pairs + lane) * cols + col)
                for col in range(cols)
                for d in held
                for lane in range(band_pairs)
            ]
        )
        held = held + [d ^ bit for d in held]
    return rounds


def within_group(value, shape, shift):
    rows, cols = shape
    band_pairs = rows // cols
    return lax.ppermute(
        value,
        "rows",
        [(row, row // band_pairs * band_pairs + (row + shift) % band_pairs) for row in range(rows)],
    )


def bulk_moves(row_piece, col_piece, corner_piece, shape):
    rows, cols = shape
    row_in = lax.ppermute(row_piece, "rows", [(r, (r + 1) % rows) for r in range(rows)])
    col_in = lax.ppermute(col_piece, "cols", [(c, (c + 1) % cols) for c in range(cols)])
    corner_in = send(
        corner_piece,
        [(r * cols + c, (r + 1) % rows * cols + (c + 1) % cols) for r in range(rows) for c in range(cols)],
    )
    return row_in, col_in, corner_in


def fill(pieces, width, tall, wide):
    return pl.pallas_call(
        functools.partial(fill_kernel, width),
        out_shape=jax.ShapeDtypeStruct((tall, wide), F32),
        in_specs=[ANY] * 4,
        out_specs=ANY,
        scratch_shapes=[pltpu.SemaphoreType.DMA((4,))],
        input_output_aliases={0: 0},
        name="fill",
    )(*pieces)


def shards(shape, matrix, gap_table, orders):
    rows, cols = shape
    band_pairs = rows // cols
    width = gap_table.shape[2]
    steps = orders.shape[0]
    tall, wide = matrix.shape
    square = jax.ShapeDtypeStruct((width, width), F32)
    stack = jax.ShapeDtypeStruct((1 + band_pairs, width, width), F32)
    group = lax.axis_index("rows") // band_pairs
    at_diagonal = group == lax.axis_index("cols")

    generator = pl.pallas_call(
        functools.partial(first_generators_kernel, shape),
        out_shape=square,
        in_specs=[ANY, ANY],
        out_specs=VMEM,
        scratch_shapes=[pltpu.VMEM((width, width), F32)] * 2 + [pltpu.SemaphoreType.DMA((2,))],
        name="first_generators",
    )(matrix, gap_table)

    inputs = (matrix,)
    sources = ((0, 0, 0, tall, wide, 0, 0),)
    for step in range(steps):
        last = step == steps - 1
        row_held, row_late = generator, None
        band_held, band_late = (generator, None) if step == 0 else (None, None)
        row_list = first_row_rounds(shape) if step == 0 else later_row_rounds(shape)
        band_list = band_rounds(shape)
        for turn in range(max(len(row_list), len(band_list)) + (step > 0)):
            band_turn = turn - (step > 0)
            if row_late is not None and turn < len(row_list):
                row_held, row_late = row_held + row_late, None
            if band_turn == 0 and step > 0:
                band_held = jnp.where(at_diagonal, row_held if row_late is None else row_held + row_late, 0.0)
            if band_late is not None:
                band_held, band_late = band_held + band_late, None
            if 0 <= band_turn < len(band_list):
                band_late = send(band_held, band_list[band_turn])
            if turn < len(row_list):
                row_late = send(row_held, row_list[turn])
        if band_late is not None:
            band_held = band_held + band_late
        band_parts = [band_held] + [within_group(band_held, shape, shift) for shift in range(1, band_pairs)]

        if last:
            generators, weights = pl.pallas_call(
                functools.partial(weights_kernel, shape),
                out_shape=(stack, stack),
                in_specs=[VMEM] * (2 + band_pairs),
                out_specs=(VMEM, VMEM),
                name="weights",
            )(row_held, row_late, *band_parts)
        else:
            if step > 0:
                matrix = fill(inputs, width, tall, wide)
                inputs, sources = (matrix,), ((0, 0, 0, tall, wide, 0, 0),)
            generators, weights, generator = pl.pallas_call(
                functools.partial(weights_and_next_kernel, shape, step),
                out_shape=(stack, stack, square),
                in_specs=[SMEM, ANY, ANY] + [VMEM] * (2 + band_pairs),
                out_specs=(VMEM, VMEM, VMEM),
                scratch_shapes=[
                    pltpu.VMEM((tall, 2 * width), F32),
                    pltpu.VMEM((width, width), F32),
                    pltpu.SemaphoreType.DMA((2,)),
                ],
                name="weights_and_next",
            )(orders, matrix, gap_table, row_held, row_late, *band_parts)
        stay_rows = width if step == 0 and not last else tall
        partial, row_piece, col_piece, corner_piece = pl.pallas_call(
            functools.partial(rotate_kernel, shape, step, sources),
            out_shape=(
                jax.ShapeDtypeStruct((stay_rows, wide), F32),
                jax.ShapeDtypeStruct((width, wide - width), F32),
                square,
                square,
            ),
            in_specs=[SMEM] + [ANY] * len(inputs) + [VMEM] * 2,
            out_specs=(VMEM,) * 4,
            scratch_shapes=[pltpu.VMEM((tall, wide), F32), pltpu.SemaphoreType.DMA((len(sources),))],
            name="rotate",
        )(orders, *inputs, generators, weights)
        row_in, col_in, corner_in = bulk_moves(row_piece, col_piece, corner_piece, shape)
        rest = wide - 2 * width
        inputs = (partial, row_in, col_in, corner_in)
        sources = (
            (0, 0, 0, width, width, 0, 0),
            (0, 0, 2 * width, width, rest, 0, 2 * width),
            (1, 0, 0, width, width, width, 0),
            (1, 0, width, width, rest, width, 2 * width),
            (2, 0, 0, width, width, 0, width),
            (3, 0, 0, width, width, width, width),
        )
    return fill(inputs, width, tall, wide)


def solution(mesh):
    shape = (mesh.shape["rows"], mesh.shape["cols"])
    in_specs = (P("rows", "cols"), P(None, "rows", None), P())
    out_specs = P("rows", "cols")
    body = functools.partial(shards, shape)
    return jax.shard_map(body, mesh=mesh, in_specs=in_specs, out_specs=out_specs, check_vma=False)
```

```python
import functools
import jax
import jax.numpy as jnp
from jax import lax
from jax.experimental import pallas as pl
from jax.experimental.pallas import tpu as pltpu
from jax.sharding import PartitionSpec as P


F32 = jnp.float32
BF16 = jnp.bfloat16
HIGHEST = lax.Precision.HIGHEST
EASY_NORM = 12.0

ANY = pl.BlockSpec(memory_space=pl.ANY)
VMEM = pl.BlockSpec(memory_space=pltpu.VMEM)
SMEM = pl.BlockSpec(memory_space=pltpu.SMEM)


def split(value):
    high = value.astype(BF16)
    low = (value - high.astype(F32)).astype(BF16)
    return high, low


def coarse_dot(left, right):
    return jnp.dot(left.astype(BF16), right.astype(BF16), preferred_element_type=F32)


def fine_dot(left, right):
    (left_high, left_low), (right_high, right_low) = left, right
    dot = functools.partial(jnp.dot, preferred_element_type=F32)
    return dot(left_high, right_high) + (dot(left_high, right_low) + dot(left_low, right_high))


def full_dot(left, right):
    return jnp.dot(left, right, precision=HIGHEST, preferred_element_type=F32)


def factors(generator, weight):
    return split(generator), split(generator.T), split(weight)


def turn_rows(first, second, parts):
    plain, flipped, weight = parts
    mixed = fine_dot(flipped, split(first)) + second
    image = 2.0 * fine_dot(weight, split(mixed))
    return first - fine_dot(plain, split(image)), image - second


def turn_columns(first, second, parts):
    plain, flipped, weight = parts
    mixed = fine_dot(split(first), plain) + second
    image = 2.0 * fine_dot(split(mixed), weight)
    return first - fine_dot(split(image), flipped), image - second


def eye(width):
    shape = (width, width)
    return (lax.broadcasted_iota(jnp.int32, shape, 0) == lax.broadcasted_iota(jnp.int32, shape, 1)).astype(F32)


def invert(generators, weights):
    count, width = generators.shape[0], generators.shape[1]
    identity = eye(width)
    every = range(count)
    flipped = [generators[q].T for q in every]
    shifted = [identity + fine_dot(split(flipped[q]), split(generators[q])) for q in every]
    bounds = [jnp.max(jnp.sum(jnp.abs(m), axis=0, keepdims=True), axis=1, keepdims=True) for m in shifted]
    worst = bounds[0]
    for bound in bounds[1:]:
        worst = jnp.maximum(worst, bound)
    norm = jnp.max(worst)

    @pl.when(norm <= EASY_NORM)
    def _():
        scale = [8.0 / (2.0 * (b + 1.0) * (b + 1.0) - (b - 1.0) * (b - 1.0)) for b in bounds]
        linear = [scale[q] * (bounds[q] + 1.0) for q in every]
        guess = [linear[q] * identity - scale[q] * shifted[q] for q in every]
        square = [coarse_dot(m, m) for m in shifted]
        rest = [identity - linear[q] * shifted[q] + scale[q] * square[q] for q in every]
        for last in (False, False, True):
            step = [coarse_dot(guess[q], rest[q]) for q in every]
            if not last:
                rest = [coarse_dot(m, m) for m in rest]
            guess = [guess[q] + step[q] for q in every]
        for _ in range(2):
            rest = [identity - fine_dot(split(shifted[q]), split(guess[q])) for q in every]
            guess = [guess[q] + coarse_dot(guess[q], rest[q]) for q in every]
        for q in every:
            weights[q] = guess[q]

    @pl.when(norm > EASY_NORM)
    def _():
        rounds = jnp.int32(10)
        for power in range(30):
            rounds += (norm > EASY_NORM * 2.0**power).astype(jnp.int32)

        def solve(q, carry):
            plain = generators[q]
            system = identity + full_dot(plain.T, plain)
            weights[q] = (2.0 / (1.0 + norm)) * identity

            def improve(_, carry):
                guess = weights[q]
                weights[q] = guess + full_dot(guess, identity - full_dot(system, guess))
                return carry

            return lax.fori_loop(0, rounds, improve, carry)

        lax.fori_loop(0, count, solve, 0)


def places(shape):
    rows, cols = shape
    band_pairs = rows // cols
    row, col = lax.axis_index("rows"), lax.axis_index("cols")
    return row, col, lax.div(row, band_pairs), lax.rem(row, band_pairs)


def copies_of(pairs, sems):
    copies = [pltpu.make_async_copy(source, target, sems.at[index]) for index, (source, target) in enumerate(pairs)]
    for copy in copies:
        copy.start()
    return copies


def wait_all(copies):
    for copy in copies:
        copy.wait()


def first_generators_kernel(shape, matrix, gap_table, out, coupling, gap, sems):
    width = out.shape[0]
    row, col, group, lane = places(shape)
    anchor = pl.multiple_of(lane * (2 * width) + width, width)
    wait_all(copies_of([(matrix.at[pl.ds(0, width), pl.ds(anchor, width)], coupling), (gap_table.at[0], gap)], sems))
    out[...] = jnp.where(group == col, coupling[...] / (2.0 * gap[...]), 0.0)


def gather_generators(shape, carried, parts, landing, generators, sems):
    band_pairs = shape[0] // shape[1]
    lane = places(shape)[3]
    pairs = [(parts[0], generators.at[0]), (parts[1], landing)]
    for shift, part in enumerate(parts[2:]):
        pairs.append((part, generators.at[1 + lax.rem(lane + carried - shift + band_pairs, band_pairs)]))
    wait_all(copies_of(pairs, sems))
    generators[0] = generators[0] + landing[...]


def weights_kernel(shape, carried, *refs):
    band_pairs = shape[0] // shape[1]
    parts, (generators, weights, landing, sems) = refs[: 2 + band_pairs], refs[2 + band_pairs :]
    gather_generators(shape, carried, parts, landing, generators, sems)
    invert(generators, weights)


def weights_and_next_kernel(shape, step, carried, *refs):
    rows, cols = shape
    band_pairs = rows // cols
    orders, matrix, own_gap, next_gap = refs[:4]
    parts = refs[4 : 6 + band_pairs]
    generators, weights, row_out, band_out, landing, block, gaps, sems, gather_sems = refs[6 + band_pairs :]
    width = landing.shape[0]
    row, col, group, lane = places(shape)
    before, after = lax.rem(row - 1 + rows, rows), lax.rem(row + 1, rows)
    pairs = []
    for index, pair in enumerate((lax.rem(before, band_pairs), lax.rem(after, band_pairs))):
        start = pl.multiple_of(pair * (2 * width), 2 * width)
        pairs.append((matrix.at[:, pl.ds(start, 2 * width)], block.at[index]))
    pairs += [(own_gap.at[step + 1], gaps.at[0]), (next_gap, gaps.at[1])]
    copies = copies_of(pairs, sems)
    gather_generators(shape, carried, parts, landing, generators, gather_sems)
    invert(generators, weights)
    wait_all(copies)

    def coupling(index, pair, row_flag, col_flag):
        first, second = block[index, :width], block[index, width:]
        top, bottom = turn_rows(first, second, factors(generators[0], weights[0]))
        picked = jnp.where(row_flag == 0, top, bottom)
        own = factors(generators[1 + pair], weights[1 + pair])
        left, right = turn_columns(picked[:, :width], picked[:, width:], own)
        return jnp.where(col_flag == 0, left, right)

    row_here, band_here = lax.div(before, band_pairs) == col, lax.div(after, band_pairs) == col

    @pl.when(row_here)
    def _():
        found = coupling(0, lax.rem(before, band_pairs), orders[step, row, 0], orders[step, before, 1])
        row_out[...] = found / (2.0 * gaps[0])

    @pl.when(jnp.logical_not(row_here))
    def _():
        row_out[...] = jnp.zeros_like(row_out)

    @pl.when(band_here)
    def _():
        found = coupling(1, lax.rem(after, band_pairs), orders[step, row, 1], orders[step, after, 0])
        band_out[...] = found.T / (2.0 * gaps[1])

    @pl.when(jnp.logical_not(band_here))
    def _():
        band_out[...] = jnp.zeros_like(band_out)


def rotate_kernel(shape, step, sources, *refs):
    count = 1 + max(source[0] for source in sources)
    orders, inputs, generators_in, weights_in = refs[0], refs[1 : 1 + count], refs[1 + count], refs[2 + count]
    stay_out, row_out, col_out, corner_out, block, generators, weights, sems = refs[3 + count :]
    width = generators.shape[1]
    band_pairs = generators.shape[0] - 1
    row, col, group, lane = places(shape)
    pairs = [(generators_in, generators), (weights_in, weights)]
    for which, source_row, source_col, rows, cols, to_row, to_col in sources:
        source = inputs[which].at[pl.ds(source_row, rows), pl.ds(source_col, cols)]
        pairs.append((source, block.at[pl.ds(to_row, rows), pl.ds(to_col, cols)]))
    copies = copies_of(pairs, sems)
    wait_all(copies[:2])
    own = factors(generators[0], weights[0])
    wait_all(copies[2:])
    keep_rows = orders[step, row, 0] == 0
    for pair in range(band_pairs):
        cols = pl.ds(pair * 2 * width, 2 * width)
        top, bottom = turn_rows(block[:width, cols], block[width:, cols], own)
        parts = factors(generators[1 + pair], weights[1 + pair])
        keep_cols = orders[step, col * band_pairs + pair, 0] == 0
        for leaves in (True, False):
            picked = jnp.where(keep_rows != leaves, top, bottom)
            left, right = turn_columns(picked[:, :width], picked[:, width:], parts)
            stay, away = jnp.where(keep_cols, left, right), jnp.where(keep_cols, right, left)
            if leaves:
                row_out[:, pl.ds(max(2 * pair - 1, 0) * width, width)] = stay
                if pair < band_pairs - 1:
                    row_out[:, pl.ds((2 * pair + 2) * width, width)] = away
                else:
                    corner_out[...] = away
            else:
                stay_out[:width, pl.ds(2 * pair * width, width)] = stay
                if pair < band_pairs - 1:
                    stay_out[:width, pl.ds((2 * pair + 3) * width, width)] = away
                else:
                    col_out[...] = away


def fill_kernel(width, partial, row_in, col_in, corner_in, out, row_mid, col_mid, corner_mid, sems):
    del partial
    wide = out.shape[1]
    inward = copies_of([(row_in, row_mid), (col_in, col_mid), (corner_in, corner_mid)], sems)
    below = out.at[pl.ds(width, width)]
    inward[0].wait()
    outward = [
        pltpu.make_async_copy(row_mid.at[:, pl.ds(0, width)], below.at[:, pl.ds(0, width)], sems.at[3]),
        pltpu.make_async_copy(
            row_mid.at[:, pl.ds(width, wide - 2 * width)], below.at[:, pl.ds(2 * width, wide - 2 * width)], sems.at[4]
        ),
        pltpu.make_async_copy(col_mid, out.at[pl.ds(0, width), pl.ds(width, width)], sems.at[5]),
        pltpu.make_async_copy(corner_mid, below.at[:, pl.ds(width, width)], sems.at[6]),
    ]
    outward[0].start()
    outward[1].start()
    inward[1].wait()
    outward[2].start()
    inward[2].wait()
    outward[3].start()
    wait_all(outward)


def send(value, pairs):
    return lax.ppermute(value, ("rows", "cols"), pairs)


def bits_below(count):
    return [1 << bit for bit in range((count - 1).bit_length())]


def row_rounds(shape, carried):
    rows, cols = shape
    band_pairs = rows // cols
    held, rounds = [0], []

    def device(row, moved):
        return row * cols + ((row - carried) % rows // band_pairs ^ moved)

    for bit in reversed(bits_below(cols)):
        rounds.append([(device(row, d), device(row, d ^ bit)) for row in range(rows) for d in held])
        held = held + [d ^ bit for d in held]
    return rounds


def band_rounds(shape, carried):
    rows, cols = shape
    band_pairs = rows // cols
    held, rounds = [0], []

    def device(col, lane, moved):
        start = (col - (carried and lane == band_pairs - 1)) % cols
        return ((start ^ moved) * band_pairs + lane) * cols + col

    for bit in reversed(bits_below(cols)):
        rounds.append(
            [
                (device(col, lane, d), device(col, lane, d ^ bit))
                for col in range(cols)
                for d in held
                for lane in range(band_pairs)
            ]
        )
        held = held + [d ^ bit for d in held]
    return rounds


def within_group(value, shape, shift):
    rows, cols = shape
    band_pairs = rows // cols
    return lax.ppermute(
        value,
        "rows",
        [(row, row // band_pairs * band_pairs + (row + shift) % band_pairs) for row in range(rows)],
    )


def bulk_moves(row_piece, col_piece, corner_piece, shape):
    rows, cols = shape
    row_in = lax.ppermute(row_piece, "rows", [(r, (r + 1) % rows) for r in range(rows)])
    col_in = lax.ppermute(col_piece, "cols", [(c, (c + 1) % cols) for c in range(cols)])
    corner_in = send(
        corner_piece,
        [(r * cols + c, (r + 1) % rows * cols + (c + 1) % cols) for r in range(rows) for c in range(cols)],
    )
    return row_in, col_in, corner_in


def fill(pieces, width, tall, wide):
    return pl.pallas_call(
        functools.partial(fill_kernel, width),
        out_shape=jax.ShapeDtypeStruct((tall, wide), F32),
        in_specs=[ANY] * 4,
        out_specs=ANY,
        scratch_shapes=[
            pltpu.VMEM((width, wide - width), F32),
            pltpu.VMEM((width, width), F32),
            pltpu.VMEM((width, width), F32),
            pltpu.SemaphoreType.DMA((7,)),
        ],
        input_output_aliases={0: 0},
        name="fill",
    )(*pieces)


def spread(row_value, band_value, shape, carried):
    row_held, band_held, row_late, band_late = row_value, band_value, None, None
    for row_pairs, band_pairs in zip(row_rounds(shape, carried), band_rounds(shape, carried)):
        if row_late is not None:
            row_held, band_held = row_held + row_late, band_held + band_late
        band_late = send(band_held, band_pairs)
        row_late = send(row_held, row_pairs)
    band_held = band_held + band_late
    lanes = shape[0] // shape[1]
    return [row_held, row_late, band_held] + [within_group(band_held, shape, shift) for shift in range(1, lanes)]


def shards(shape, matrix, gap_table, orders):
    rows, cols = shape
    band_pairs = rows // cols
    width = gap_table.shape[2]
    steps = orders.shape[0]
    tall, wide = matrix.shape
    square = jax.ShapeDtypeStruct((width, width), F32)
    stack = jax.ShapeDtypeStruct((1 + band_pairs, width, width), F32)
    dma = pltpu.SemaphoreType.DMA

    row_value = pl.pallas_call(
        functools.partial(first_generators_kernel, shape),
        out_shape=square,
        in_specs=[ANY, ANY],
        out_specs=VMEM,
        scratch_shapes=[pltpu.VMEM((width, width), F32)] * 2 + [dma((2,))],
        name="first_generators",
    )(matrix, gap_table)
    band_value = row_value

    inputs = (matrix,)
    sources = ((0, 0, 0, tall, wide, 0, 0),)
    for step in range(steps):
        last = step == steps - 1
        carried = int(step > 0)
        parts = spread(row_value, band_value, shape, carried)
        if last:
            generators, weights = pl.pallas_call(
                functools.partial(weights_kernel, shape, carried),
                out_shape=(stack, stack),
                in_specs=[ANY] * (2 + band_pairs),
                out_specs=(VMEM, VMEM),
                scratch_shapes=[pltpu.VMEM((width, width), F32), dma((2 + band_pairs,))],
                name="weights",
            )(*parts)
        else:
            if step > 0:
                matrix = fill(inputs, width, tall, wide)
                inputs, sources = (matrix,), ((0, 0, 0, tall, wide, 0, 0),)
            wanted = [
                ((row + 1) % rows * cols + (row + 1) % rows // band_pairs, row * cols + (row + 1) % rows // band_pairs)
                for row in range(rows)
            ]
            next_gap = send(gap_table[step + 1], wanted)
            generators, weights, row_value, band_value = pl.pallas_call(
                functools.partial(weights_and_next_kernel, shape, step, carried),
                out_shape=(stack, stack, square, square),
                in_specs=[SMEM, ANY, ANY, ANY] + [ANY] * (2 + band_pairs),
                out_specs=(VMEM, VMEM, VMEM, VMEM),
                scratch_shapes=[
                    pltpu.VMEM((width, width), F32),
                    pltpu.VMEM((2, tall, 2 * width), F32),
                    pltpu.VMEM((2, width, width), F32),
                    dma((4,)),
                    dma((2 + band_pairs,)),
                ],
                name="weights_and_next",
            )(orders, matrix, gap_table, next_gap, *parts)
        stay_rows = width if step == 0 and not last else tall
        pieces = pl.pallas_call(
            functools.partial(rotate_kernel, shape, step, sources),
            out_shape=(
                jax.ShapeDtypeStruct((stay_rows, wide), F32),
                jax.ShapeDtypeStruct((width, wide - width), F32),
                square,
                square,
            ),
            in_specs=[SMEM] + [ANY] * len(inputs) + [ANY] * 2,
            out_specs=(VMEM,) * 4,
            scratch_shapes=[
                pltpu.VMEM((tall, wide), F32),
                pltpu.VMEM(stack.shape, F32),
                pltpu.VMEM(stack.shape, F32),
                dma((len(sources) + 2,)),
            ],
            name="rotate",
        )(orders, *inputs, generators, weights)
        inputs = (pieces[0], *bulk_moves(*pieces[1:], shape))
        rest = wide - 2 * width
        sources = (
            (0, 0, 0, width, width, 0, 0),
            (0, 0, 2 * width, width, rest, 0, 2 * width),
            (1, 0, 0, width, width, width, 0),
            (1, 0, width, width, rest, width, 2 * width),
            (2, 0, 0, width, width, 0, width),
            (3, 0, 0, width, width, width, width),
        )
    return fill(inputs, width, tall, wide)


def solution(mesh):
    shape = (mesh.shape["rows"], mesh.shape["cols"])
    in_specs = (P("rows", "cols"), P(None, "rows", None), P())
    out_specs = P("rows", "cols")
    body = functools.partial(shards, shape)
    return jax.shard_map(body, mesh=mesh, in_specs=in_specs, out_specs=out_specs, check_vma=False)
```

```python
import functools
import jax
import jax.numpy as jnp
from jax import lax
from jax.experimental import pallas as pl
from jax.experimental.pallas import tpu as pltpu
from jax.sharding import PartitionSpec as P


F32 = jnp.float32
BF16 = jnp.bfloat16
HIGHEST = lax.Precision.HIGHEST
EASY_NORM = 8.0
KERNEL_BYTES = 20 << 20

ANY = pl.BlockSpec(memory_space=pl.ANY)
VMEM = pl.BlockSpec(memory_space=pltpu.VMEM)
SMEM = pl.BlockSpec(memory_space=pltpu.SMEM)


def split(value):
    high = value.astype(BF16)
    low = (value - high.astype(F32)).astype(BF16)
    return high, low


def coarse_dot(left, right):
    return jnp.dot(left.astype(BF16), right.astype(BF16), preferred_element_type=F32)


def fine_dot(left, right):
    (left_high, left_low), (right_high, right_low) = left, right
    wide = jnp.concatenate([left_high, left_high, left_low], axis=1)
    tall = jnp.concatenate([right_high, right_low, right_high], axis=0)
    return jnp.dot(wide, tall, preferred_element_type=F32)


def full_dot(left, right):
    return jnp.dot(left, right, precision=HIGHEST, preferred_element_type=F32)


def factors(ref, index):
    return tuple((ref[index, 2 * part], ref[index, 2 * part + 1]) for part in range(3))


def turn_rows(first, second, parts):
    plain, flipped, weight = parts
    mixed = fine_dot(flipped, split(first)) + second
    image = 2.0 * fine_dot(weight, split(mixed))
    return first - fine_dot(plain, split(image)), image - second


def turn_columns(first, second, parts):
    plain, flipped, weight = parts
    mixed = fine_dot(split(first), plain) + second
    image = 2.0 * fine_dot(split(mixed), weight)
    return first - fine_dot(split(image), flipped), image - second


def eye(width):
    shape = (width, width)
    return (lax.broadcasted_iota(jnp.int32, shape, 0) == lax.broadcasted_iota(jnp.int32, shape, 1)).astype(F32)


def row_sums(value):
    return jnp.max(jnp.sum(jnp.abs(value), axis=0, keepdims=True), axis=1, keepdims=True)


def invert(generators, weights):
    count, width = generators.shape[0], generators.shape[1]
    identity = eye(width)
    every = range(count)
    shifted = [identity + fine_dot(split(generators[q].T), split(generators[q])) for q in every]
    square = [coarse_dot(m, m) for m in shifted]
    bounds = [jnp.sqrt(row_sums(square[q]) + 0.01 * row_sums(shifted[q]) ** 2) for q in every]
    worst = bounds[0]
    for bound in bounds[1:]:
        worst = jnp.maximum(worst, bound)
    norm = jnp.max(worst)

    @pl.when(norm <= EASY_NORM)
    def _():
        guess, rest, grow = [], [], []
        for q in every:
            bound = jnp.maximum(bounds[q], 1.25)
            ratio = (bound + 1.0) / (bound - 1.0)
            two = 2.0 * ratio * ratio - 1.0
            four = 2.0 * two * two - 1.0
            eight = 2.0 * four * four - 1.0
            scale = 8.0 / (two * (bound - 1.0) * (bound - 1.0))
            guess.append((scale * (bound + 1.0)) * identity - scale * shifted[q])
            rest.append(identity - (scale * (bound + 1.0)) * shifted[q] + scale * square[q])
            grow.append((2.0 * two * two / four, 1.0 / four, 2.0 * four * four / eight))
        both = [coarse_dot(jnp.concatenate([guess[q], rest[q]], axis=0), rest[q]) for q in every]
        guess = [grow[q][0] * (guess[q] + both[q][:width]) for q in every]
        rest = [grow[q][0] * both[q][width:] - grow[q][1] * identity for q in every]
        step = [coarse_dot(guess[q], rest[q]) for q in every]
        guess = [grow[q][2] * (guess[q] + step[q]) for q in every]
        rest = [identity - fine_dot(split(shifted[q]), split(guess[q])) for q in every]
        for q in every:
            weights[q] = guess[q] + coarse_dot(guess[q], rest[q])

    @pl.when(norm > EASY_NORM)
    def _():
        rounds = jnp.int32(10)
        for power in range(30):
            rounds += (norm > EASY_NORM * 2.0**power).astype(jnp.int32)

        def solve(q, carry):
            plain = generators[q]
            system = identity + full_dot(plain.T, plain)
            weights[q] = (2.0 / (1.0 + jnp.max(row_sums(system)))) * identity

            def improve(_, carry):
                guess = weights[q]
                weights[q] = guess + full_dot(guess, identity - full_dot(system, guess))
                return carry

            return lax.fori_loop(0, rounds, improve, carry)

        lax.fori_loop(0, count, solve, 0)


def places(shape):
    rows, cols = shape
    band_pairs = rows // cols
    row, col = lax.axis_index("rows"), lax.axis_index("cols")
    return row, col, lax.div(row, band_pairs), lax.rem(row, band_pairs)


def copies_of(pairs, sems):
    copies = [pltpu.make_async_copy(source, target, sems.at[index]) for index, (source, target) in enumerate(pairs)]
    for copy in copies:
        copy.start()
    return copies


def wait_all(copies):
    for copy in copies:
        copy.wait()


def first_generators_kernel(shape, matrix, gap_table, out, coupling, gap, sems):
    width = out.shape[0]
    row, col, group, lane = places(shape)
    anchor = pl.multiple_of(lane * (2 * width) + width, width)
    wait_all(copies_of([(matrix.at[pl.ds(0, width), pl.ds(anchor, width)], coupling), (gap_table.at[0], gap)], sems))
    out[...] = jnp.where(group == col, coupling[...] / (2.0 * gap[...]), 0.0)


def find_factors(shape, carried, parts, factor_out, generators, weights):
    band_pairs = shape[0] // shape[1]
    lane = places(shape)[3]
    generators[0] = parts[0][...] + parts[1][...]
    for shift, part in enumerate(parts[2:]):
        generators[1 + lax.rem(lane + carried - shift + band_pairs, band_pairs)] = part[...]
    invert(generators, weights)
    for index in range(1 + band_pairs):
        plain = generators[index]
        for part, value in enumerate((plain, plain.T, weights[index])):
            factor_out[index, 2 * part], factor_out[index, 2 * part + 1] = split(value)


def weights_kernel(shape, carried, *refs):
    find_factors(shape, carried, refs[:-3], *refs[-3:])


def weights_and_next_kernel(shape, step, carried, *refs):
    rows, cols = shape
    band_pairs = rows // cols
    orders, matrix, own_gap, next_gap = refs[:4]
    factor_out, row_out, band_out, generators, weights = refs[6 + band_pairs :]
    width = row_out.shape[0]
    row, col, group, lane = places(shape)
    before, after = lax.rem(row - 1 + rows, rows), lax.rem(row + 1, rows)
    find_factors(shape, carried, refs[4 : 6 + band_pairs], factor_out, generators, weights)

    def coupling(pair, row_flag, col_flag):
        cols = pl.ds(pl.multiple_of(pair * (2 * width), 2 * width), 2 * width)
        top, bottom = turn_rows(matrix[:width, cols], matrix[width:, cols], factors(factor_out, 0))
        picked = jnp.where(row_flag == 0, top, bottom)
        left, right = turn_columns(picked[:, :width], picked[:, width:], factors(factor_out, 1 + pair))
        return jnp.where(col_flag == 0, left, right)

    row_here, band_here = lax.div(before, band_pairs) == col, lax.div(after, band_pairs) == col

    @pl.when(row_here)
    def _():
        found = coupling(lax.rem(before, band_pairs), orders[step, row, 0], orders[step, before, 1])
        row_out[...] = found / (2.0 * own_gap[step + 1])

    @pl.when(jnp.logical_not(row_here))
    def _():
        row_out[...] = jnp.zeros_like(row_out)

    @pl.when(band_here)
    def _():
        found = coupling(lax.rem(after, band_pairs), orders[step, row, 1], orders[step, after, 0])
        band_out[...] = found.T / (2.0 * next_gap[...])

    @pl.when(jnp.logical_not(band_here))
    def _():
        band_out[...] = jnp.zeros_like(band_out)


def rotate_kernel(shape, step, pairs, quarters, *refs):
    count = 1 + max(quarter[0] for corners in quarters for quarter in corners)
    orders, factor_in, outputs = refs[0], refs[1 + count], refs[2 + count :]
    band_pairs = shape[0] // shape[1]
    width = factor_in.shape[2]
    row, col, group, lane = places(shape)
    own = factors(factor_in, 0)
    keep_rows = orders[step, row, 0] == 0
    for index, (pair, corners) in enumerate(zip(pairs, quarters)):
        tiles = [refs[1 + which][pl.ds(at_row, width), pl.ds(at_col, width)] for which, at_row, at_col in corners]
        first, second = jnp.concatenate(tiles[:2], axis=1), jnp.concatenate(tiles[2:], axis=1)
        top, bottom = turn_rows(first, second, own)
        parts = factors(factor_in, 1 + pair)
        keep_cols = orders[step, col * band_pairs + pair, 0] == 0
        for leaves in (0, 1):
            picked = jnp.where(keep_rows, bottom, top) if leaves else jnp.where(keep_rows, top, bottom)
            left, right = turn_columns(picked[:, :width], picked[:, width:], parts)
            stay, away = jnp.where(keep_cols, left, right), jnp.where(keep_cols, right, left)
            if pair == band_pairs - 1:
                outputs[leaves][...], outputs[2 + leaves][...] = stay, away
            else:
                outputs[leaves][:, pl.ds(2 * index * width, width)] = stay
                outputs[leaves][:, pl.ds((2 * index + 1) * width, width)] = away


def local_fill_kernel(width, last_stay, others, out, sems):
    band = others.shape[1] // (2 * width)
    moves = [(last_stay, 2 * band)]
    for pair in range(band):
        moves.append((others.at[:, pl.ds(2 * pair * width, width)], 2 * pair))
        moves.append((others.at[:, pl.ds((2 * pair + 1) * width, width)], 2 * pair + 3))
    wait_all(copies_of([(source, out.at[pl.ds(0, width), pl.ds(slot * width, width)]) for source, slot in moves], sems))


def fill_kernel(width, partial, last_in, others_in, col_in, corner_in, out, sems):
    del partial
    band = others_in.shape[1] // (2 * width)
    moves = [(col_in, 0, 1), (corner_in, width, 1), (last_in, width, 2 * band)]
    for pair in range(band):
        moves.append((others_in.at[:, pl.ds(2 * pair * width, width)], width, 2 * pair))
        moves.append((others_in.at[:, pl.ds((2 * pair + 1) * width, width)], width, 2 * pair + 3))
    wait_all(
        copies_of(
            [(source, out.at[pl.ds(at_row, width), pl.ds(slot * width, width)]) for source, at_row, slot in moves], sems
        )
    )


def send(value, pairs):
    return lax.ppermute(value, ("rows", "cols"), pairs)


def bits_below(count):
    return [1 << bit for bit in range((count - 1).bit_length())]


def row_rounds(shape, carried):
    rows, cols = shape
    band_pairs = rows // cols
    held, rounds = [0], []

    def device(row, moved):
        return row * cols + ((row - carried) % rows // band_pairs ^ moved)

    for bit in reversed(bits_below(cols)):
        rounds.append([(device(row, d), device(row, d ^ bit)) for row in range(rows) for d in held])
        held = held + [d ^ bit for d in held]
    return rounds


def band_rounds(shape, carried):
    rows, cols = shape
    band_pairs = rows // cols
    held, rounds = [0], []

    def device(col, lane, moved):
        start = (col - (carried and lane == band_pairs - 1)) % cols
        return ((start ^ moved) * band_pairs + lane) * cols + col

    for bit in reversed(bits_below(cols)):
        rounds.append(
            [
                (device(col, lane, d), device(col, lane, d ^ bit))
                for col in range(cols)
                for d in held
                for lane in range(band_pairs)
            ]
        )
        held = held + [d ^ bit for d in held]
    return rounds


def within_group(value, shape, shift):
    rows, cols = shape
    band_pairs = rows // cols
    return lax.ppermute(
        value,
        "rows",
        [(row, row // band_pairs * band_pairs + (row + shift) % band_pairs) for row in range(rows)],
    )


def to_next_rows(value, shape):
    return lax.ppermute(value, "rows", [(r, (r + 1) % shape[0]) for r in range(shape[0])])


def to_next_cols(value, shape):
    return lax.ppermute(value, "cols", [(c, (c + 1) % shape[1]) for c in range(shape[1])])


def to_next_corner(value, shape):
    rows, cols = shape
    return send(
        value, [(r * cols + c, (r + 1) % rows * cols + (c + 1) % cols) for r in range(rows) for c in range(cols)]
    )


def on_chip(value):
    return pltpu.with_memory_space_constraint(value, pltpu.VMEM)


def call(kernel, name, outputs, operands, scratch=(), specs=None, **settings):
    specs = specs or {}
    operands = [value if index in specs else on_chip(value) for index, value in enumerate(operands)]
    return pl.pallas_call(
        kernel,
        out_shape=outputs,
        in_specs=[specs.get(index, VMEM) for index in range(len(operands))],
        out_specs=settings.pop("out_specs", jax.tree.map(lambda _: VMEM, outputs)),
        scratch_shapes=list(scratch),
        compiler_params=pltpu.CompilerParams(vmem_limit_bytes=KERNEL_BYTES),
        name=name,
        **settings,
    )(*operands)


def spread(row_value, band_value, shape, carried):
    row_held, band_held, row_late, band_late = row_value, band_value, None, None
    for row_pairs, band_pairs in zip(row_rounds(shape, carried), band_rounds(shape, carried)):
        if row_late is not None:
            row_held, band_held = row_held + row_late, band_held + band_late
        band_late = send(band_held, band_pairs)
        row_late = send(row_held, row_pairs)
    band_held = band_held + band_late
    lanes = shape[0] // shape[1]
    return [row_held, row_late, band_held] + [within_group(band_held, shape, shift) for shift in range(1, lanes)]


def finish(pieces, width, tall, wide):
    last_stay, others, last_in, others_in, col_in, corner_in = pieces
    result = jax.ShapeDtypeStruct((tall, wide), F32)
    count = wide // width
    partial = call(
        functools.partial(local_fill_kernel, width),
        "fill_local",
        result,
        (last_stay, others),
        [pltpu.SemaphoreType.DMA((count,))],
        out_specs=ANY,
    )
    return call(
        functools.partial(fill_kernel, width),
        "fill",
        result,
        (partial, last_in, others_in, col_in, corner_in),
        [pltpu.SemaphoreType.DMA((count + 2,))],
        specs={0: ANY},
        out_specs=ANY,
        input_output_aliases={0: 0},
    )


def shards(shape, matrix, gap_table, orders):
    rows, cols = shape
    band_pairs = rows // cols
    width = gap_table.shape[2]
    steps = orders.shape[0]
    tall, wide = matrix.shape
    square = pltpu.VMEM((width, width), F32)
    many = pltpu.VMEM((width, wide - 2 * width), F32)
    stack = pltpu.VMEM((1 + band_pairs, width, width), F32)
    split_stack = pltpu.VMEM((1 + band_pairs, 6, width, width), BF16)
    dma = pltpu.SemaphoreType.DMA

    row_value = call(
        functools.partial(first_generators_kernel, shape),
        "first_generators",
        square,
        (matrix, gap_table),
        [square, square, dma((2,))],
        specs={0: ANY, 1: ANY},
    )
    band_value = row_value

    last_pair = band_pairs - 1
    for step in range(steps):
        carried = int(step > 0)
        parts = spread(row_value, band_value, shape, carried)
        if step == steps - 1:
            split_factors = call(
                functools.partial(weights_kernel, shape, carried), "weights", split_stack, parts, [stack, stack]
            )
        else:
            if step > 0:
                matrix = finish(pieces, width, tall, wide)
            wanted = [
                ((row + 1) % rows * cols + (row + 1) % rows // band_pairs, row * cols + (row + 1) % rows // band_pairs)
                for row in range(rows)
            ]
            next_gap = send(gap_table[step + 1], wanted)
            split_factors, row_value, band_value = call(
                functools.partial(weights_and_next_kernel, shape, step, carried),
                "weights_and_next",
                (split_stack, square, square),
                (orders, matrix, gap_table, next_gap, *parts),
                [stack, stack],
                specs={0: SMEM},
            )
        if step < steps - 1 or steps == 1:
            tiles = lambda pair: tuple((0, i * width, (2 * pair + j) * width) for i in (0, 1) for j in (0, 1))
            last_inputs, last_tiles = (matrix,), (tiles(last_pair),)
            other_inputs, other_tiles = (matrix,), tuple(tiles(pair) for pair in range(last_pair))
        else:
            last_stay, others, last_in, others_in, col_in, corner_in = pieces
            last_inputs = (last_stay, others, last_in, others_in)
            edge = (2 * last_pair - 1) * width
            last_tiles = (((0, 0, 0), (1, 0, edge), (2, 0, 0), (3, 0, edge)),)
            other_inputs = (others, others_in, col_in, corner_in)
            other_tiles = tuple(
                tuple(
                    (side, 0, 2 * pair * width) if slot == 0 else (side, 0, (2 * pair - 1) * width) if pair else (2 + side, 0, 0)
                    for side in (0, 1)
                    for slot in (0, 1)
                )
                for pair in range(last_pair)
            )
        last_stay, last_leave, col_piece, corner_piece = call(
            functools.partial(rotate_kernel, shape, step, (last_pair,), last_tiles),
            "rotate_last",
            (square,) * 4,
            (orders, *last_inputs, split_factors),
            specs={0: SMEM},
        )
        col_in, corner_in = to_next_cols(col_piece, shape), to_next_corner(corner_piece, shape)
        last_in = to_next_rows(last_leave, shape)
        others, others_leave = call(
            functools.partial(rotate_kernel, shape, step, tuple(range(last_pair)), other_tiles),
            "rotate_others",
            (many, many),
            (orders, *other_inputs, split_factors),
            specs={0: SMEM},
        )
        others_in = to_next_rows(others_leave, shape)
        pieces = (last_stay, others, last_in, others_in, col_in, corner_in)
    return finish(pieces, width, tall, wide)


def solution(mesh):
    shape = (mesh.shape["rows"], mesh.shape["cols"])
    in_specs = (P("rows", "cols"), P(None, "rows", None), P())
    out_specs = P("rows", "cols")
    body = functools.partial(shards, shape)
    return jax.shard_map(body, mesh=mesh, in_specs=in_specs, out_specs=out_specs, check_vma=False)
```

```python
import functools
import jax
import jax.numpy as jnp
from jax import lax
from jax.experimental import pallas as pl
from jax.experimental.pallas import tpu as pltpu
from jax.sharding import PartitionSpec as P


F32 = jnp.float32
BF16 = jnp.bfloat16
HIGHEST = lax.Precision.HIGHEST
EASY_NORM = 8.0
KERNEL_BYTES = 20 << 20

ANY = pl.BlockSpec(memory_space=pl.ANY)
VMEM = pl.BlockSpec(memory_space=pltpu.VMEM)
SMEM = pl.BlockSpec(memory_space=pltpu.SMEM)
HBM = pl.BlockSpec(memory_space=pltpu.HBM)


def split(value):
    high = value.astype(BF16)
    low = (value - high.astype(F32)).astype(BF16)
    return high, low


def coarse_dot(left, right):
    return jnp.dot(left.astype(BF16), right.astype(BF16), preferred_element_type=F32)


def fine_dot(left, right):
    (left_high, left_low), (right_high, right_low) = left, right
    wide = jnp.concatenate([left_high, left_high, left_low], axis=1)
    tall = jnp.concatenate([right_high, right_low, right_high], axis=0)
    return jnp.dot(wide, tall, preferred_element_type=F32)


def full_dot(left, right):
    return jnp.dot(left, right, precision=HIGHEST, preferred_element_type=F32)


def factors(ref, index):
    return tuple((ref[index, 2 * part], ref[index, 2 * part + 1]) for part in range(3))


def turn_rows(first, second, parts):
    plain, flipped, weight = parts
    mixed = fine_dot(flipped, split(first)) + second
    image = 2.0 * fine_dot(weight, split(mixed))
    return first - fine_dot(plain, split(image)), image - second


def turn_columns(first, second, parts):
    plain, flipped, weight = parts
    mixed = fine_dot(split(first), plain) + second
    image = 2.0 * fine_dot(split(mixed), weight)
    return first - fine_dot(split(image), flipped), image - second


def eye(width):
    shape = (width, width)
    return (lax.broadcasted_iota(jnp.int32, shape, 0) == lax.broadcasted_iota(jnp.int32, shape, 1)).astype(F32)


def row_sums(value):
    return jnp.max(jnp.sum(jnp.abs(value), axis=0, keepdims=True), axis=1, keepdims=True)


def invert(generators, weights):
    count, width = generators.shape[0], generators.shape[1]
    identity = eye(width)
    every = range(count)
    shifted = [identity + fine_dot(split(generators[q].T), split(generators[q])) for q in every]
    square = [coarse_dot(m, m) for m in shifted]
    bounds = [jnp.sqrt(row_sums(square[q]) + 0.01 * row_sums(shifted[q]) ** 2) for q in every]
    worst = bounds[0]
    for bound in bounds[1:]:
        worst = jnp.maximum(worst, bound)
    norm = jnp.max(worst)

    @pl.when(norm <= EASY_NORM)
    def _():
        guess, rest, grow = [], [], []
        for q in every:
            bound = jnp.maximum(bounds[q], 1.25)
            ratio = (bound + 1.0) / (bound - 1.0)
            two = 2.0 * ratio * ratio - 1.0
            four = 2.0 * two * two - 1.0
            eight = 2.0 * four * four - 1.0
            scale = 8.0 / (two * (bound - 1.0) * (bound - 1.0))
            guess.append((scale * (bound + 1.0)) * identity - scale * shifted[q])
            rest.append(identity - (scale * (bound + 1.0)) * shifted[q] + scale * square[q])
            grow.append((2.0 * two * two / four, 1.0 / four, 2.0 * four * four / eight))
        both = [coarse_dot(jnp.concatenate([guess[q], rest[q]], axis=0), rest[q]) for q in every]
        guess = [grow[q][0] * (guess[q] + both[q][:width]) for q in every]
        rest = [grow[q][0] * both[q][width:] - grow[q][1] * identity for q in every]
        step = [coarse_dot(guess[q], rest[q]) for q in every]
        guess = [grow[q][2] * (guess[q] + step[q]) for q in every]
        rest = [identity - fine_dot(split(shifted[q]), split(guess[q])) for q in every]
        for q in every:
            weights[q] = guess[q] + coarse_dot(guess[q], rest[q])

    @pl.when(norm > EASY_NORM)
    def _():
        rounds = jnp.int32(10)
        for power in range(30):
            rounds += (norm > EASY_NORM * 2.0**power).astype(jnp.int32)

        def solve(q, carry):
            plain = generators[q]
            system = identity + full_dot(plain.T, plain)
            weights[q] = (2.0 / (1.0 + jnp.max(row_sums(system)))) * identity

            def improve(_, carry):
                guess = weights[q]
                weights[q] = guess + full_dot(guess, identity - full_dot(system, guess))
                return carry

            return lax.fori_loop(0, rounds, improve, carry)

        lax.fori_loop(0, count, solve, 0)


def places(shape):
    rows, cols = shape
    band_pairs = rows // cols
    row, col = lax.axis_index("rows"), lax.axis_index("cols")
    return row, col, lax.div(row, band_pairs), lax.rem(row, band_pairs)


def copies_of(pairs, sems):
    copies = [pltpu.make_async_copy(source, target, sems.at[index]) for index, (source, target) in enumerate(pairs)]
    for copy in copies:
        copy.start()
    return copies


def wait_all(copies):
    for copy in copies:
        copy.wait()


def first_generators_kernel(shape, matrix, gap_table, out, coupling, gap, sems):
    width = out.shape[0]
    _, col, group, lane = places(shape)
    anchor = pl.multiple_of(lane * (2 * width) + width, width)
    wait_all(copies_of([(matrix.at[pl.ds(0, width), pl.ds(anchor, width)], coupling), (gap_table.at[0], gap)], sems))
    out[...] = jnp.where(group == col, coupling[...] / (2.0 * gap[...]), 0.0)


def find_factors(shape, carried, parts, factor_out, generators, weights):
    band_pairs = shape[0] // shape[1]
    lane = places(shape)[3]
    generators[0] = parts[0][...] + parts[1][...]
    for shift, part in enumerate(parts[2:]):
        generators[1 + lax.rem(lane + carried - shift + band_pairs, band_pairs)] = part[...]
    invert(generators, weights)
    for index in range(1 + band_pairs):
        plain = generators[index]
        for part, value in enumerate((plain, plain.T, weights[index])):
            factor_out[index, 2 * part], factor_out[index, 2 * part + 1] = split(value)


def weights_kernel(shape, carried, *refs):
    find_factors(shape, carried, refs[:-3], *refs[-3:])


def weights_and_next_kernel(shape, step, carried, *refs):
    rows, cols = shape
    band_pairs = rows // cols
    orders, matrix, own_gap, next_gap = refs[:4]
    factor_out, row_out, band_out, generators, weights = refs[6 + band_pairs :]
    width = row_out.shape[0]
    row, col, _, _ = places(shape)
    before, after = lax.rem(row - 1 + rows, rows), lax.rem(row + 1, rows)
    find_factors(shape, carried, refs[4 : 6 + band_pairs], factor_out, generators, weights)

    def coupling(pair, row_flag, col_flag):
        cols = pl.ds(pl.multiple_of(pair * (2 * width), 2 * width), 2 * width)
        top, bottom = turn_rows(matrix[:width, cols], matrix[width:, cols], factors(factor_out, 0))
        picked = jnp.where(row_flag == 0, top, bottom)
        left, right = turn_columns(picked[:, :width], picked[:, width:], factors(factor_out, 1 + pair))
        return jnp.where(col_flag == 0, left, right)

    row_here, band_here = lax.div(before, band_pairs) == col, lax.div(after, band_pairs) == col

    @pl.when(row_here)
    def _():
        found = coupling(lax.rem(before, band_pairs), orders[step, row, 0], orders[step, before, 1])
        row_out[...] = found / (2.0 * own_gap[step + 1])

    @pl.when(jnp.logical_not(row_here))
    def _():
        row_out[...] = jnp.zeros_like(row_out)

    @pl.when(band_here)
    def _():
        found = coupling(lax.rem(after, band_pairs), orders[step, row, 1], orders[step, after, 0])
        band_out[...] = found.T / (2.0 * next_gap[...])

    @pl.when(jnp.logical_not(band_here))
    def _():
        band_out[...] = jnp.zeros_like(band_out)


def rotate_kernel(shape, step, pairs, quarters, *refs):
    count = 1 + max(quarter[0] for corners in quarters for quarter in corners)
    orders, factor_in, outputs = refs[0], refs[1 + count], refs[2 + count :]
    band_pairs = shape[0] // shape[1]
    width = factor_in.shape[2]
    row, col, _, _ = places(shape)
    own = factors(factor_in, 0)
    keep_rows = orders[step, row, 0] == 0
    for index, (pair, corners) in enumerate(zip(pairs, quarters)):
        tiles = [refs[1 + which][pl.ds(at_row, width), pl.ds(at_col, width)] for which, at_row, at_col in corners]
        first, second = jnp.concatenate(tiles[:2], axis=1), jnp.concatenate(tiles[2:], axis=1)
        top, bottom = turn_rows(first, second, own)
        parts = factors(factor_in, 1 + pair)
        keep_cols = orders[step, col * band_pairs + pair, 0] == 0
        for leaves in (0, 1):
            picked = jnp.where(keep_rows, bottom, top) if leaves else jnp.where(keep_rows, top, bottom)
            left, right = turn_columns(picked[:, :width], picked[:, width:], parts)
            stay, away = jnp.where(keep_cols, left, right), jnp.where(keep_cols, right, left)
            if pair == band_pairs - 1:
                outputs[leaves][...], outputs[2 + leaves][...] = stay, away
            else:
                outputs[leaves][:, pl.ds(2 * index * width, width)] = stay
                outputs[leaves][:, pl.ds((2 * index + 1) * width, width)] = away


def local_fill_kernel(width, last_stay, others, out, sems):
    band = others.shape[1] // (2 * width)
    moves = [(last_stay, 2 * band)]
    for pair in range(band):
        moves.append((others.at[:, pl.ds(2 * pair * width, width)], 2 * pair))
        moves.append((others.at[:, pl.ds((2 * pair + 1) * width, width)], 2 * pair + 3))
    wait_all(copies_of([(source, out.at[pl.ds(0, width), pl.ds(slot * width, width)]) for source, slot in moves], sems))


def fill_kernel(width, partial, last_in, others_in, col_in, corner_in, out, sems):
    del partial
    band = others_in.shape[1] // (2 * width)
    moves = [(col_in, 0, 1), (corner_in, width, 1), (last_in, width, 2 * band)]
    for pair in range(band):
        moves.append((others_in.at[:, pl.ds(2 * pair * width, width)], width, 2 * pair))
        moves.append((others_in.at[:, pl.ds((2 * pair + 1) * width, width)], width, 2 * pair + 3))
    wait_all(
        copies_of(
            [(source, out.at[pl.ds(at_row, width), pl.ds(slot * width, width)]) for source, at_row, slot in moves], sems
        )
    )


def send(value, pairs):
    return lax.ppermute(value, ("rows", "cols"), pairs)


def bits_below(count):
    return [1 << bit for bit in range((count - 1).bit_length())]


def row_rounds(shape, carried):
    rows, cols = shape
    band_pairs = rows // cols
    held, rounds = [0], []

    def device(row, moved):
        return row * cols + ((row - carried) % rows // band_pairs ^ moved)

    for bit in reversed(bits_below(cols)):
        rounds.append([(device(row, d), device(row, d ^ bit)) for row in range(rows) for d in held])
        held = held + [d ^ bit for d in held]
    return rounds


def band_rounds(shape, carried):
    rows, cols = shape
    band_pairs = rows // cols
    held, rounds = [0], []

    def device(col, lane, moved):
        start = (col - (carried and lane == band_pairs - 1)) % cols
        return ((start ^ moved) * band_pairs + lane) * cols + col

    for bit in bits_below(cols) if carried else reversed(bits_below(cols)):
        rounds.append(
            [
                (device(col, lane, d), device(col, lane, d ^ bit))
                for col in range(cols)
                for d in held
                for lane in range(band_pairs)
            ]
        )
        held = held + [d ^ bit for d in held]
    return rounds


def within_group(value, shape, shift):
    rows, cols = shape
    band_pairs = rows // cols
    return lax.ppermute(
        value,
        "rows",
        [(row, row // band_pairs * band_pairs + (row + shift) % band_pairs) for row in range(rows)],
    )


def to_next_rows(value, shape):
    return lax.ppermute(value, "rows", [(r, (r + 1) % shape[0]) for r in range(shape[0])])


def to_next_cols(value, shape):
    return lax.ppermute(value, "cols", [(c, (c + 1) % shape[1]) for c in range(shape[1])])


def to_next_corner(value, shape):
    rows, cols = shape
    return send(
        value, [(r * cols + c, (r + 1) % rows * cols + (c + 1) % cols) for r in range(rows) for c in range(cols)]
    )


def placed(value, space):
    return value if space is None else pltpu.with_memory_space_constraint(value, space)


def call(kernel, outputs, operands, scratch=(), specs=None, **settings):
    specs = specs or {}
    spaces = {id(SMEM): None, id(ANY): None, id(HBM): pltpu.HBM}
    operands = [placed(value, spaces[id(specs[index])] if index in specs else pltpu.VMEM) for index, value in enumerate(operands)]
    return pl.pallas_call(
        kernel,
        out_shape=outputs,
        in_specs=[specs.get(index, VMEM) for index in range(len(operands))],
        out_specs=settings.pop("out_specs", jax.tree.map(lambda _: VMEM, outputs)),
        scratch_shapes=list(scratch),
        compiler_params=pltpu.CompilerParams(vmem_limit_bytes=KERNEL_BYTES),
        **settings,
    )(*operands)


def spread(row_value, band_value, shape, carried):
    row_held, band_held, row_late, band_late = row_value, band_value, None, None
    for row_pairs, band_pairs in zip(row_rounds(shape, carried), band_rounds(shape, carried)):
        if row_late is not None:
            row_held, band_held = row_held + row_late, band_held + band_late
        band_late = send(band_held, band_pairs)
        row_late = send(row_held, row_pairs)
    band_held = band_held + band_late
    lanes = shape[0] // shape[1]
    return [row_held, row_late, band_held] + [within_group(band_held, shape, shift) for shift in range(1, lanes)]


def finish(pieces, width, tall, wide):
    last_stay, others, last_in, others_in, col_in, corner_in = pieces
    result = jax.ShapeDtypeStruct((tall, wide), F32)
    count = wide // width
    partial = call(
        functools.partial(local_fill_kernel, width),
        result,
        (last_stay, others),
        [pltpu.SemaphoreType.DMA((count,))],
        out_specs=ANY,
    )
    return call(
        functools.partial(fill_kernel, width),
        result,
        (partial, last_in, others_in, col_in, corner_in),
        [pltpu.SemaphoreType.DMA((count + 2,))],
        specs={0: ANY},
        out_specs=ANY,
        input_output_aliases={0: 0},
    )


def shards(shape, matrix, gap_table, orders):
    rows, cols = shape
    band_pairs = rows // cols
    width = gap_table.shape[2]
    steps = orders.shape[0]
    tall, wide = matrix.shape
    square = pltpu.VMEM((width, width), F32)
    many = pltpu.VMEM((width, wide - 2 * width), F32)
    stack = pltpu.VMEM((1 + band_pairs, width, width), F32)
    split_stack = pltpu.VMEM((1 + band_pairs, 6, width, width), BF16)
    dma = pltpu.SemaphoreType.DMA

    row_value = call(
        functools.partial(first_generators_kernel, shape),
        square,
        (matrix, gap_table),
        [square, square, dma((2,))],
        specs={0: HBM, 1: HBM},
    )
    band_value = row_value

    last_pair = band_pairs - 1
    for step in range(steps):
        carried = int(step > 0)
        parts = spread(row_value, band_value, shape, carried)
        if step == steps - 1:
            split_factors = call(functools.partial(weights_kernel, shape, carried), split_stack, parts, [stack, stack])
        else:
            if step > 0:
                matrix = finish(pieces, width, tall, wide)
            wanted = [
                ((row + 1) % rows * cols + (row + 1) % rows // band_pairs, row * cols + (row + 1) % rows // band_pairs)
                for row in range(rows)
            ]
            next_gap = send(gap_table[step + 1], wanted)
            split_factors, row_value, band_value = call(
                functools.partial(weights_and_next_kernel, shape, step, carried),
                (split_stack, square, square),
                (orders, matrix, gap_table, next_gap, *parts),
                [stack, stack],
                specs={0: SMEM},
            )
        if step < steps - 1 or steps == 1:
            tiles = lambda pair: tuple((0, i * width, (2 * pair + j) * width) for i in (0, 1) for j in (0, 1))
            last_inputs, last_tiles = (matrix,), (tiles(last_pair),)
            other_inputs, other_tiles = (matrix,), tuple(tiles(pair) for pair in range(last_pair))
        else:
            last_stay, others, last_in, others_in, col_in, corner_in = pieces
            last_inputs = (last_stay, others, last_in, others_in)
            edge = (2 * last_pair - 1) * width
            last_tiles = (((0, 0, 0), (1, 0, edge), (2, 0, 0), (3, 0, edge)),)
            other_inputs = (others, others_in, col_in, corner_in)
            other_tiles = tuple(
                tuple(
                    (side, 0, 2 * pair * width) if slot == 0 else (side, 0, (2 * pair - 1) * width) if pair else (2 + side, 0, 0)
                    for side in (0, 1)
                    for slot in (0, 1)
                )
                for pair in range(last_pair)
            )
        last_stay, last_leave, col_piece, corner_piece = call(
            functools.partial(rotate_kernel, shape, step, (last_pair,), last_tiles),
            (square,) * 4,
            (orders, *last_inputs, split_factors),
            specs={0: SMEM},
        )
        others, others_leave = call(
            functools.partial(rotate_kernel, shape, step, tuple(range(last_pair)), other_tiles),
            (many, many),
            (orders, *other_inputs, split_factors),
            specs={0: SMEM},
        )
        col_in = to_next_cols(col_piece, shape)
        corner_in = to_next_corner(corner_piece, shape)
        last_in = to_next_rows(last_leave, shape)
        others_in = to_next_rows(others_leave, shape)
        pieces = (last_stay, others, last_in, others_in, col_in, corner_in)
    return finish(pieces, width, tall, wide)


def solution(mesh):
    shape = (mesh.shape["rows"], mesh.shape["cols"])
    in_specs = (P("rows", "cols"), P(None, "rows", None), P())
    out_specs = P("rows", "cols")

    def body(matrix, gap_table, orders):
        return shards(shape, matrix, gap_table, orders)

    return jax.shard_map(body, mesh=mesh, in_specs=in_specs, out_specs=out_specs, check_vma=False)
```

```python
import functools
import jax
import jax.numpy as jnp
from jax import lax
from jax.experimental import pallas as pl
from jax.experimental.pallas import tpu as pltpu
from jax.sharding import PartitionSpec as P


F32 = jnp.float32
BF16 = jnp.bfloat16
HIGHEST = lax.Precision.HIGHEST
EASY_NORM = 8.0
KERNEL_BYTES = 20 << 20

ANY = pl.BlockSpec(memory_space=pl.ANY)
VMEM = pl.BlockSpec(memory_space=pltpu.VMEM)
SMEM = pl.BlockSpec(memory_space=pltpu.SMEM)
HBM = pl.BlockSpec(memory_space=pltpu.HBM)


def split(value):
    high = value.astype(BF16)
    low = (value - high.astype(F32)).astype(BF16)
    return high, low


def coarse_dot(left, right):
    return jnp.dot(left.astype(BF16), right.astype(BF16), preferred_element_type=F32)


def fine_dot(left, right):
    (left_high, left_low), (right_high, right_low) = left, right
    wide = jnp.concatenate([left_high, left_high, left_low], axis=1)
    tall = jnp.concatenate([right_high, right_low, right_high], axis=0)
    return jnp.dot(wide, tall, preferred_element_type=F32)


def full_dot(left, right):
    return jnp.dot(left, right, precision=HIGHEST, preferred_element_type=F32)


def factors(ref, index):
    return tuple((ref[index, 2 * part], ref[index, 2 * part + 1]) for part in range(3))


def turn_rows(first, second, parts):
    plain, flipped, weight = parts
    mixed = fine_dot(flipped, split(first)) + second
    image = 2.0 * fine_dot(weight, split(mixed))
    return first - fine_dot(plain, split(image)), image - second


def turn_columns(first, second, parts):
    plain, flipped, weight = parts
    mixed = fine_dot(split(first), plain) + second
    image = 2.0 * fine_dot(split(mixed), weight)
    return first - fine_dot(split(image), flipped), image - second


def eye(width):
    shape = (width, width)
    return (lax.broadcasted_iota(jnp.int32, shape, 0) == lax.broadcasted_iota(jnp.int32, shape, 1)).astype(F32)


def row_sums(value):
    return jnp.max(jnp.sum(jnp.abs(value), axis=0, keepdims=True), axis=1, keepdims=True)


def invert(generators, weights):
    count, width = generators.shape[0], generators.shape[1]
    identity = eye(width)
    every = range(count)
    shifted = [identity + fine_dot(split(generators[q].T), split(generators[q])) for q in every]
    square = [coarse_dot(m, m) for m in shifted]
    bounds = [jnp.sqrt(row_sums(square[q]) + 0.01 * row_sums(shifted[q]) ** 2) for q in every]
    worst = bounds[0]
    for bound in bounds[1:]:
        worst = jnp.maximum(worst, bound)
    norm = jnp.max(worst)

    @pl.when(norm <= EASY_NORM)
    def _():
        guess, rest, grow = [], [], []
        for q in every:
            bound = jnp.maximum(bounds[q], 1.25)
            ratio = (bound + 1.0) / (bound - 1.0)
            two = 2.0 * ratio * ratio - 1.0
            four = 2.0 * two * two - 1.0
            eight = 2.0 * four * four - 1.0
            scale = 8.0 / (two * (bound - 1.0) * (bound - 1.0))
            guess.append((scale * (bound + 1.0)) * identity - scale * shifted[q])
            rest.append(identity - (scale * (bound + 1.0)) * shifted[q] + scale * square[q])
            grow.append((2.0 * two * two / four, 1.0 / four, 2.0 * four * four / eight))
        both = [coarse_dot(jnp.concatenate([guess[q], rest[q]], axis=0), rest[q]) for q in every]
        guess = [grow[q][0] * (guess[q] + both[q][:width]) for q in every]
        rest = [grow[q][0] * both[q][width:] - grow[q][1] * identity for q in every]
        step = [coarse_dot(guess[q], rest[q]) for q in every]
        guess = [grow[q][2] * (guess[q] + step[q]) for q in every]
        rest = [identity - fine_dot(split(shifted[q]), split(guess[q])) for q in every]
        for q in every:
            weights[q] = guess[q] + coarse_dot(guess[q], rest[q])

    @pl.when(norm > EASY_NORM)
    def _():
        rounds = jnp.int32(10)
        for power in range(30):
            rounds += (norm > EASY_NORM * 2.0**power).astype(jnp.int32)

        def solve(q, carry):
            plain = generators[q]
            system = identity + full_dot(plain.T, plain)
            weights[q] = (2.0 / (1.0 + jnp.max(row_sums(system)))) * identity

            def improve(_, carry):
                guess = weights[q]
                weights[q] = guess + full_dot(guess, identity - full_dot(system, guess))
                return carry

            return lax.fori_loop(0, rounds, improve, carry)

        lax.fori_loop(0, count, solve, 0)


def places(shape):
    rows, cols = shape
    band_pairs = rows // cols
    row, col = lax.axis_index("rows"), lax.axis_index("cols")
    return row, col, lax.div(row, band_pairs), lax.rem(row, band_pairs)


def copies_of(pairs, sems):
    copies = [pltpu.make_async_copy(source, target, sems.at[index]) for index, (source, target) in enumerate(pairs)]
    for copy in copies:
        copy.start()
    return copies


def wait_all(copies):
    for copy in copies:
        copy.wait()


def first_generators_kernel(shape, matrix, gap_table, out, coupling, gap, sems):
    width = out.shape[0]
    _, col, group, lane = places(shape)
    anchor = pl.multiple_of(lane * (2 * width) + width, width)
    wait_all(copies_of([(matrix.at[pl.ds(0, width), pl.ds(anchor, width)], coupling), (gap_table.at[0], gap)], sems))
    out[...] = jnp.where(group == col, coupling[...] / (2.0 * gap[...]), 0.0)


def find_factors(shape, carried, parts, factor_out, generators, weights):
    band_pairs = shape[0] // shape[1]
    lane = places(shape)[3]
    generators[0] = parts[0][...] + parts[1][...]
    for shift, part in enumerate(parts[2:]):
        generators[1 + lax.rem(lane + carried - shift + band_pairs, band_pairs)] = part[...]
    invert(generators, weights)
    for index in range(1 + band_pairs):
        plain = generators[index]
        for part, value in enumerate((plain, plain.T, weights[index])):
            factor_out[index, 2 * part], factor_out[index, 2 * part + 1] = split(value)


def weights_kernel(shape, carried, *refs):
    find_factors(shape, carried, refs[:-3], *refs[-3:])


def weights_and_next_kernel(shape, step, carried, *refs):
    rows, cols = shape
    band_pairs = rows // cols
    orders, matrix, own_gap, next_gap = refs[:4]
    factor_out, row_out, band_out, generators, weights = refs[6 + band_pairs :]
    width = row_out.shape[0]
    row, col, _, _ = places(shape)
    before, after = lax.rem(row - 1 + rows, rows), lax.rem(row + 1, rows)
    find_factors(shape, carried, refs[4 : 6 + band_pairs], factor_out, generators, weights)

    def coupling(pair, row_flag, col_flag):
        cols = pl.ds(pl.multiple_of(pair * (2 * width), 2 * width), 2 * width)
        top, bottom = turn_rows(matrix[:width, cols], matrix[width:, cols], factors(factor_out, 0))
        picked = jnp.where(row_flag == 0, top, bottom)
        left, right = turn_columns(picked[:, :width], picked[:, width:], factors(factor_out, 1 + pair))
        return jnp.where(col_flag == 0, left, right)

    row_here, band_here = lax.div(before, band_pairs) == col, lax.div(after, band_pairs) == col

    @pl.when(row_here)
    def _():
        found = coupling(lax.rem(before, band_pairs), orders[step, row, 0], orders[step, before, 1])
        row_out[...] = found / (2.0 * own_gap[step + 1])

    @pl.when(jnp.logical_not(row_here))
    def _():
        row_out[...] = jnp.zeros_like(row_out)

    @pl.when(band_here)
    def _():
        found = coupling(lax.rem(after, band_pairs), orders[step, row, 1], orders[step, after, 0])
        band_out[...] = found.T / (2.0 * next_gap[...])

    @pl.when(jnp.logical_not(band_here))
    def _():
        band_out[...] = jnp.zeros_like(band_out)


def rotate_kernel(shape, step, pairs, quarters, *refs):
    count = 1 + max(quarter[0] for corners in quarters for quarter in corners)
    orders, factor_in, outputs = refs[0], refs[1 + count], refs[2 + count :]
    band_pairs = shape[0] // shape[1]
    width = factor_in.shape[2]
    row, col, _, _ = places(shape)
    own = factors(factor_in, 0)
    keep_rows = orders[step, row, 0] == 0
    for index, (pair, corners) in enumerate(zip(pairs, quarters)):
        tiles = [refs[1 + which][pl.ds(at_row, width), pl.ds(at_col, width)] for which, at_row, at_col in corners]
        first, second = jnp.concatenate(tiles[:2], axis=1), jnp.concatenate(tiles[2:], axis=1)
        top, bottom = turn_rows(first, second, own)
        parts = factors(factor_in, 1 + pair)
        keep_cols = orders[step, col * band_pairs + pair, 0] == 0
        first = jnp.concatenate([top[:, :width], bottom[:, :width]], axis=0)
        second = jnp.concatenate([top[:, width:], bottom[:, width:]], axis=0)
        left, right = turn_columns(first, second, parts)
        stay, away = jnp.where(keep_cols, left, right), jnp.where(keep_cols, right, left)
        for leaves in (0, 1):
            keep = jnp.logical_not(keep_rows) if leaves else keep_rows
            stay_rows = jnp.where(keep, stay[:width], stay[width:])
            away_rows = jnp.where(keep, away[:width], away[width:])
            if pair == band_pairs - 1:
                outputs[leaves][...], outputs[2 + leaves][...] = stay_rows, away_rows
            else:
                outputs[leaves][:, pl.ds(2 * index * width, width)] = stay_rows
                outputs[leaves][:, pl.ds((2 * index + 1) * width, width)] = away_rows


def local_fill_kernel(width, last_stay, others, out, sems):
    band = others.shape[1] // (2 * width)
    moves = [(last_stay, 2 * band)]
    for pair in range(band):
        moves.append((others.at[:, pl.ds(2 * pair * width, width)], 2 * pair))
        moves.append((others.at[:, pl.ds((2 * pair + 1) * width, width)], 2 * pair + 3))
    wait_all(copies_of([(source, out.at[pl.ds(0, width), pl.ds(slot * width, width)]) for source, slot in moves], sems))


def fill_kernel(width, partial, last_in, others_in, col_in, corner_in, out, sems):
    del partial
    band = others_in.shape[1] // (2 * width)
    moves = [(col_in, 0, 1), (corner_in, width, 1), (last_in, width, 2 * band)]
    for pair in range(band):
        moves.append((others_in.at[:, pl.ds(2 * pair * width, width)], width, 2 * pair))
        moves.append((others_in.at[:, pl.ds((2 * pair + 1) * width, width)], width, 2 * pair + 3))
    wait_all(
        copies_of(
            [(source, out.at[pl.ds(at_row, width), pl.ds(slot * width, width)]) for source, at_row, slot in moves], sems
        )
    )


def send(value, pairs):
    return lax.ppermute(value, ("rows", "cols"), pairs)


def bits_below(count):
    return [1 << bit for bit in range((count - 1).bit_length())]


def row_rounds(shape, carried):
    rows, cols = shape
    band_pairs = rows // cols
    held, rounds = [0], []

    def device(row, moved):
        return row * cols + ((row - carried) % rows // band_pairs ^ moved)

    for bit in reversed(bits_below(cols)):
        rounds.append([(device(row, d), device(row, d ^ bit)) for row in range(rows) for d in held])
        held = held + [d ^ bit for d in held]
    return rounds


def band_rounds(shape, carried):
    rows, cols = shape
    band_pairs = rows // cols
    bits = bits_below(cols)
    rounds = [[] for _ in bits]
    for lane in range(band_pairs):
        order = bits[lane % len(bits) :] + bits[: lane % len(bits)]
        for col in range(cols):
            start = (col - (carried and lane == band_pairs - 1)) % cols
            held = [start]
            for pairs, bit in zip(rounds, order):
                pairs.extend(((g * band_pairs + lane) * cols + col, ((g ^ bit) * band_pairs + lane) * cols + col) for g in held)
                held = held + [g ^ bit for g in held]
    return rounds


def within_group(value, shape, shift):
    rows, cols = shape
    band_pairs = rows // cols
    return lax.ppermute(
        value,
        "rows",
        [(row, row // band_pairs * band_pairs + (row + shift) % band_pairs) for row in range(rows)],
    )


def to_next_rows(value, shape):
    return lax.ppermute(value, "rows", [(r, (r + 1) % shape[0]) for r in range(shape[0])])


def to_next_cols(value, shape):
    return lax.ppermute(value, "cols", [(c, (c + 1) % shape[1]) for c in range(shape[1])])


def to_next_corner(value, shape):
    rows, cols = shape
    return send(
        value, [(r * cols + c, (r + 1) % rows * cols + (c + 1) % cols) for r in range(rows) for c in range(cols)]
    )


def placed(value, space):
    return value if space is None else pltpu.with_memory_space_constraint(value, space)


def call(kernel, outputs, operands, scratch=(), specs=None, **settings):
    specs = specs or {}
    spaces = {id(SMEM): None, id(ANY): None, id(HBM): pltpu.HBM}
    operands = [placed(value, spaces[id(specs[index])] if index in specs else pltpu.VMEM) for index, value in enumerate(operands)]
    return pl.pallas_call(
        kernel,
        out_shape=outputs,
        in_specs=[specs.get(index, VMEM) for index in range(len(operands))],
        out_specs=settings.pop("out_specs", jax.tree.map(lambda _: VMEM, outputs)),
        scratch_shapes=list(scratch),
        compiler_params=pltpu.CompilerParams(vmem_limit_bytes=KERNEL_BYTES),
        **settings,
    )(*operands)


def spread(row_value, band_value, shape, carried):
    row_held, band_held, row_late, band_late = row_value, band_value, None, None
    for row_pairs, band_pairs in zip(row_rounds(shape, carried), band_rounds(shape, carried)):
        if row_late is not None:
            row_held, band_held = row_held + row_late, band_held + band_late
        band_late = send(band_held, band_pairs)
        row_late = send(row_held, row_pairs)
    band_held = band_held + band_late
    lanes = shape[0] // shape[1]
    return [row_held, row_late, band_held] + [within_group(band_held, shape, shift) for shift in range(1, lanes)]


def finish(pieces, width, tall, wide):
    last_stay, others, last_in, others_in, col_in, corner_in = pieces
    result = jax.ShapeDtypeStruct((tall, wide), F32)
    count = wide // width
    partial = call(
        functools.partial(local_fill_kernel, width),
        result,
        (last_stay, others),
        [pltpu.SemaphoreType.DMA((count,))],
        out_specs=ANY,
    )
    return call(
        functools.partial(fill_kernel, width),
        result,
        (partial, last_in, others_in, col_in, corner_in),
        [pltpu.SemaphoreType.DMA((count + 2,))],
        specs={0: ANY},
        out_specs=ANY,
        input_output_aliases={0: 0},
    )


def shards(shape, matrix, gap_table, orders):
    rows, cols = shape
    band_pairs = rows // cols
    width = gap_table.shape[2]
    steps = orders.shape[0]
    tall, wide = matrix.shape
    square = pltpu.VMEM((width, width), F32)
    many = pltpu.VMEM((width, wide - 2 * width), F32)
    stack = pltpu.VMEM((1 + band_pairs, width, width), F32)
    split_stack = pltpu.VMEM((1 + band_pairs, 6, width, width), BF16)
    dma = pltpu.SemaphoreType.DMA

    row_value = call(
        functools.partial(first_generators_kernel, shape),
        square,
        (matrix, gap_table),
        [square, square, dma((2,))],
        specs={0: HBM, 1: HBM},
    )
    band_value = lax.optimization_barrier(row_value)

    last_pair = band_pairs - 1
    for step in range(steps):
        carried = int(step > 0)
        parts = spread(row_value, band_value, shape, carried)
        if step == steps - 1:
            split_factors = call(functools.partial(weights_kernel, shape, carried), split_stack, parts, [stack, stack])
        else:
            if step > 0:
                matrix = finish(pieces, width, tall, wide)
            wanted = [
                ((row + 1) % rows * cols + (row + 1) % rows // band_pairs, row * cols + (row + 1) % rows // band_pairs)
                for row in range(rows)
            ]
            next_gap = send(gap_table[step + 1], wanted)
            split_factors, row_value, band_value = call(
                functools.partial(weights_and_next_kernel, shape, step, carried),
                (split_stack, square, square),
                (orders, matrix, gap_table, next_gap, *parts),
                [stack, stack],
                specs={0: SMEM},
            )
        if step < steps - 1 or steps == 1:
            tiles = lambda pair: tuple((0, i * width, (2 * pair + j) * width) for i in (0, 1) for j in (0, 1))
            last_inputs, last_tiles = (matrix,), (tiles(last_pair),)
            other_inputs, other_tiles = (matrix,), tuple(tiles(pair) for pair in range(last_pair))
        else:
            last_stay, others, last_in, others_in, col_in, corner_in = pieces
            last_inputs = (last_stay, others, last_in, others_in)
            edge = (2 * last_pair - 1) * width
            last_tiles = (((0, 0, 0), (1, 0, edge), (2, 0, 0), (3, 0, edge)),)
            other_inputs = (others, others_in, col_in, corner_in)
            other_tiles = tuple(
                tuple(
                    (side, 0, 2 * pair * width) if slot == 0 else (side, 0, (2 * pair - 1) * width) if pair else (2 + side, 0, 0)
                    for side in (0, 1)
                    for slot in (0, 1)
                )
                for pair in range(last_pair)
            )
        last_stay, last_leave, col_piece, corner_piece = call(
            functools.partial(rotate_kernel, shape, step, (last_pair,), last_tiles),
            (square,) * 4,
            (orders, *last_inputs, split_factors),
            specs={0: SMEM},
        )
        others, others_leave = call(
            functools.partial(rotate_kernel, shape, step, tuple(range(last_pair)), other_tiles),
            (many, many),
            (orders, *other_inputs, split_factors),
            specs={0: SMEM},
        )
        col_in = to_next_cols(col_piece, shape)
        corner_in = to_next_corner(corner_piece, shape)
        last_in = to_next_rows(last_leave, shape)
        others_in = to_next_rows(others_leave, shape)
        pieces = (last_stay, others, last_in, others_in, col_in, corner_in)
    return finish(pieces, width, tall, wide)


def solution(mesh):
    shape = (mesh.shape["rows"], mesh.shape["cols"])
    in_specs = (P("rows", "cols"), P(None, "rows", None), P())
    out_specs = P("rows", "cols")

    def body(matrix, gap_table, orders):
        return shards(shape, matrix, gap_table, orders)

    return jax.shard_map(body, mesh=mesh, in_specs=in_specs, out_specs=out_specs, check_vma=False)
```

```python
import functools
import jax
import jax.numpy as jnp
from jax import lax
from jax.experimental import pallas as pl
from jax.experimental.pallas import tpu as pltpu
from jax.sharding import PartitionSpec as P


F32 = jnp.float32
BF16 = jnp.bfloat16
HIGHEST = lax.Precision.HIGHEST
EASY_NORM = 8.0
KERNEL_BYTES = 20 << 20

ANY = pl.BlockSpec(memory_space=pl.ANY)
VMEM = pl.BlockSpec(memory_space=pltpu.VMEM)
SMEM = pl.BlockSpec(memory_space=pltpu.SMEM)
HBM = pl.BlockSpec(memory_space=pltpu.HBM)


def split(value):
    high = value.astype(BF16)
    low = (value - high.astype(F32)).astype(BF16)
    return high, low


def coarse_dot(left, right):
    return jnp.dot(left.astype(BF16), right.astype(BF16), preferred_element_type=F32)


def fine_dot(left, right):
    (left_high, left_low), (right_high, right_low) = left, right
    wide = jnp.concatenate([left_high, left_high, left_low], axis=1)
    tall = jnp.concatenate([right_high, right_low, right_high], axis=0)
    return jnp.dot(wide, tall, preferred_element_type=F32)


def full_dot(left, right):
    return jnp.dot(left, right, precision=HIGHEST, preferred_element_type=F32)


def factors(ref, index):
    return tuple((ref[index, 2 * part], ref[index, 2 * part + 1]) for part in range(3))


def turn_rows(first, second, parts):
    plain, flipped, weight = parts
    mixed = fine_dot(flipped, split(first)) + second
    image = 2.0 * fine_dot(weight, split(mixed))
    return first - fine_dot(plain, split(image)), image - second


def turn_columns(first, second, parts):
    plain, flipped, weight = parts
    mixed = fine_dot(split(first), plain) + second
    image = 2.0 * fine_dot(split(mixed), weight)
    return first - fine_dot(split(image), flipped), image - second


def eye(width):
    shape = (width, width)
    return (lax.broadcasted_iota(jnp.int32, shape, 0) == lax.broadcasted_iota(jnp.int32, shape, 1)).astype(F32)


def row_sums(value):
    return jnp.max(jnp.sum(jnp.abs(value), axis=0, keepdims=True), axis=1, keepdims=True)


def invert(generators, weights):
    count, width = generators.shape[0], generators.shape[1]
    identity = eye(width)
    every = range(count)
    shifted = [identity + fine_dot(split(generators[q].T), split(generators[q])) for q in every]
    square = [coarse_dot(m, m) for m in shifted]
    bounds = [jnp.sqrt(row_sums(square[q]) + 0.01 * row_sums(shifted[q]) ** 2) for q in every]
    worst = bounds[0]
    for bound in bounds[1:]:
        worst = jnp.maximum(worst, bound)
    norm = jnp.max(worst)

    @pl.when(norm <= EASY_NORM)
    def _():
        guess, rest, grow = [], [], []
        for q in every:
            bound = jnp.maximum(bounds[q], 1.25)
            ratio = (bound + 1.0) / (bound - 1.0)
            two = 2.0 * ratio * ratio - 1.0
            four = 2.0 * two * two - 1.0
            eight = 2.0 * four * four - 1.0
            scale = 8.0 / (two * (bound - 1.0) * (bound - 1.0))
            guess.append((scale * (bound + 1.0)) * identity - scale * shifted[q])
            rest.append(identity - (scale * (bound + 1.0)) * shifted[q] + scale * square[q])
            grow.append((2.0 * two * two / four, 1.0 / four, 2.0 * four * four / eight))
        both = [coarse_dot(jnp.concatenate([guess[q], rest[q]], axis=0), rest[q]) for q in every]
        guess = [grow[q][0] * (guess[q] + both[q][:width]) for q in every]
        rest = [grow[q][0] * both[q][width:] - grow[q][1] * identity for q in every]
        step = [coarse_dot(guess[q], rest[q]) for q in every]
        guess = [grow[q][2] * (guess[q] + step[q]) for q in every]
        rest = [identity - fine_dot(split(shifted[q]), split(guess[q])) for q in every]
        for q in every:
            weights[q] = guess[q] + coarse_dot(guess[q], rest[q])

    @pl.when(norm > EASY_NORM)
    def _():
        rounds = jnp.int32(10)
        for power in range(30):
            rounds += (norm > EASY_NORM * 2.0**power).astype(jnp.int32)

        def solve(q, carry):
            plain = generators[q]
            system = identity + full_dot(plain.T, plain)
            weights[q] = (2.0 / (1.0 + jnp.max(row_sums(system)))) * identity

            def improve(_, carry):
                guess = weights[q]
                weights[q] = guess + full_dot(guess, identity - full_dot(system, guess))
                return carry

            return lax.fori_loop(0, rounds, improve, carry)

        lax.fori_loop(0, count, solve, 0)


def places(shape):
    rows, cols = shape
    band_pairs = rows // cols
    row, col = lax.axis_index("rows"), lax.axis_index("cols")
    return row, col, lax.div(row, band_pairs), lax.rem(row, band_pairs)


def copies_of(pairs, sems):
    copies = [pltpu.make_async_copy(source, target, sems.at[index]) for index, (source, target) in enumerate(pairs)]
    for copy in copies:
        copy.start()
    return copies


def wait_all(copies):
    for copy in copies:
        copy.wait()


def first_generators_kernel(shape, matrix, gap_table, out, coupling, gap, sems):
    width = out.shape[0]
    _, col, group, lane = places(shape)
    anchor = pl.multiple_of(lane * (2 * width) + width, width)
    wait_all(copies_of([(matrix.at[pl.ds(0, width), pl.ds(anchor, width)], coupling), (gap_table.at[0], gap)], sems))
    out[...] = jnp.where(group == col, coupling[...] / (2.0 * gap[...]), 0.0)


def write_factors(generators, weights, targets):
    for index, (target, place) in enumerate(targets):
        plain = generators[index]
        for part, value in enumerate((plain, plain.T, weights[index])):
            target[place, 2 * part], target[place, 2 * part + 1] = split(value)


def order_band(shape, carried, band_parts, generators, first):
    band_pairs = shape[0] // shape[1]
    lane = places(shape)[3]
    for shift, part in enumerate(band_parts):
        generators[first + lax.rem(lane + carried - shift + band_pairs, band_pairs)] = part[...]


def band_weights_kernel(shape, carried, *refs):
    band_parts, (band_out, generators, weights) = refs[:-3], refs[-3:]
    order_band(shape, carried, band_parts, generators, 0)
    invert(generators, weights)
    write_factors(generators, weights, [(band_out, pair) for pair in range(len(band_parts))])


def weights_kernel(shape, carried, *refs):
    row_parts, band_parts, (row_out, band_out, generators, weights) = refs[:2], refs[2:-4], refs[-4:]
    generators[0] = row_parts[0][...] + row_parts[1][...]
    order_band(shape, carried, band_parts, generators, 1)
    invert(generators, weights)
    write_factors(generators, weights, [(row_out, 0)] + [(band_out, pair) for pair in range(len(band_parts))])


def row_weights_and_next_kernel(shape, step, *refs):
    rows, cols = shape
    band_pairs = rows // cols
    orders, matrix, own_gap, next_gap, band_in, first_part, second_part = refs[:7]
    row_factors, row_out, band_out, generators, weights = refs[7:]
    width = row_out.shape[0]
    row, col, _, _ = places(shape)
    before, after = lax.rem(row - 1 + rows, rows), lax.rem(row + 1, rows)
    generators[0] = first_part[...] + second_part[...]
    invert(generators, weights)
    write_factors(generators, weights, [(row_factors, 0)])

    def coupling(pair, row_flag, col_flag):
        cols = pl.ds(pl.multiple_of(pair * (2 * width), 2 * width), 2 * width)
        top, bottom = turn_rows(matrix[:width, cols], matrix[width:, cols], factors(row_factors, 0))
        picked = jnp.where(row_flag == 0, top, bottom)
        left, right = turn_columns(picked[:, :width], picked[:, width:], factors(band_in, pair))
        return jnp.where(col_flag == 0, left, right)

    row_here, band_here = lax.div(before, band_pairs) == col, lax.div(after, band_pairs) == col

    @pl.when(row_here)
    def _():
        found = coupling(lax.rem(before, band_pairs), orders[step, row, 0], orders[step, before, 1])
        row_out[...] = found / (2.0 * own_gap[step + 1])

    @pl.when(jnp.logical_not(row_here))
    def _():
        row_out[...] = jnp.zeros_like(row_out)

    @pl.when(band_here)
    def _():
        found = coupling(lax.rem(after, band_pairs), orders[step, row, 1], orders[step, after, 0])
        band_out[...] = found.T / (2.0 * next_gap[...])

    @pl.when(jnp.logical_not(band_here))
    def _():
        band_out[...] = jnp.zeros_like(band_out)


def rotate_kernel(shape, step, pairs, quarters, *refs):
    count = 1 + max(quarter[0] for corners in quarters for quarter in corners)
    orders, row_factors, factor_in, outputs = refs[0], refs[1 + count], refs[2 + count], refs[3 + count :]
    band_pairs = shape[0] // shape[1]
    width = factor_in.shape[2]
    row, col, _, _ = places(shape)
    own = factors(row_factors, 0)
    keep_rows = orders[step, row, 0] == 0
    for index, (pair, corners) in enumerate(zip(pairs, quarters)):
        tiles = [refs[1 + which][pl.ds(at_row, width), pl.ds(at_col, width)] for which, at_row, at_col in corners]
        first, second = jnp.concatenate(tiles[:2], axis=1), jnp.concatenate(tiles[2:], axis=1)
        top, bottom = turn_rows(first, second, own)
        parts = factors(factor_in, pair)
        keep_cols = orders[step, col * band_pairs + pair, 0] == 0
        first = jnp.concatenate([top[:, :width], bottom[:, :width]], axis=0)
        second = jnp.concatenate([top[:, width:], bottom[:, width:]], axis=0)
        left, right = turn_columns(first, second, parts)
        stay, away = jnp.where(keep_cols, left, right), jnp.where(keep_cols, right, left)
        for leaves in (0, 1):
            keep = jnp.logical_not(keep_rows) if leaves else keep_rows
            stay_rows = jnp.where(keep, stay[:width], stay[width:])
            away_rows = jnp.where(keep, away[:width], away[width:])
            if pair == band_pairs - 1:
                outputs[leaves][...], outputs[2 + leaves][...] = stay_rows, away_rows
            else:
                outputs[leaves][:, pl.ds(2 * index * width, width)] = stay_rows
                outputs[leaves][:, pl.ds((2 * index + 1) * width, width)] = away_rows


def local_fill_kernel(width, last_stay, others, out, sems):
    band = others.shape[1] // (2 * width)
    moves = [(last_stay, 2 * band)]
    for pair in range(band):
        moves.append((others.at[:, pl.ds(2 * pair * width, width)], 2 * pair))
        moves.append((others.at[:, pl.ds((2 * pair + 1) * width, width)], 2 * pair + 3))
    wait_all(copies_of([(source, out.at[pl.ds(0, width), pl.ds(slot * width, width)]) for source, slot in moves], sems))


def fill_kernel(width, partial, last_in, others_in, col_in, corner_in, out, sems):
    del partial
    band = others_in.shape[1] // (2 * width)
    moves = [(col_in, 0, 1), (corner_in, width, 1), (last_in, width, 2 * band)]
    for pair in range(band):
        moves.append((others_in.at[:, pl.ds(2 * pair * width, width)], width, 2 * pair))
        moves.append((others_in.at[:, pl.ds((2 * pair + 1) * width, width)], width, 2 * pair + 3))
    wait_all(
        copies_of(
            [(source, out.at[pl.ds(at_row, width), pl.ds(slot * width, width)]) for source, at_row, slot in moves], sems
        )
    )


def send(value, pairs):
    return lax.ppermute(value, ("rows", "cols"), pairs)


def bits_below(count):
    return [1 << bit for bit in range((count - 1).bit_length())]


def row_rounds(shape, carried):
    rows, cols = shape
    band_pairs = rows // cols
    held, rounds = [0], []

    def device(row, moved):
        return row * cols + ((row - carried) % rows // band_pairs ^ moved)

    for bit in reversed(bits_below(cols)):
        rounds.append([(device(row, d), device(row, d ^ bit)) for row in range(rows) for d in held])
        held = held + [d ^ bit for d in held]
    return rounds


def band_rounds(shape, carried):
    rows, cols = shape
    band_pairs = rows // cols
    bits = bits_below(cols)
    rounds = [[] for _ in bits]
    for lane in range(band_pairs):
        order = bits[lane % len(bits) :] + bits[: lane % len(bits)]
        for col in range(cols):
            start = (col - (carried and lane == band_pairs - 1)) % cols
            held = [start]
            for pairs, bit in zip(rounds, order):
                pairs.extend(((g * band_pairs + lane) * cols + col, ((g ^ bit) * band_pairs + lane) * cols + col) for g in held)
                held = held + [g ^ bit for g in held]
    return rounds


def within_group(value, shape, shift):
    rows, cols = shape
    band_pairs = rows // cols
    return lax.ppermute(
        value,
        "rows",
        [(row, row // band_pairs * band_pairs + (row + shift) % band_pairs) for row in range(rows)],
    )


def to_next_rows(value, shape):
    return lax.ppermute(value, "rows", [(r, (r + 1) % shape[0]) for r in range(shape[0])])


def to_next_cols(value, shape):
    return lax.ppermute(value, "cols", [(c, (c + 1) % shape[1]) for c in range(shape[1])])


def to_next_corner(value, shape):
    rows, cols = shape
    return send(
        value, [(r * cols + c, (r + 1) % rows * cols + (c + 1) % cols) for r in range(rows) for c in range(cols)]
    )


def placed(value, space):
    return value if space is None else pltpu.with_memory_space_constraint(value, space)


def call(kernel, outputs, operands, scratch=(), specs=None, **settings):
    specs = specs or {}
    spaces = {id(SMEM): None, id(ANY): None, id(HBM): pltpu.HBM}
    operands = [placed(value, spaces[id(specs[index])] if index in specs else pltpu.VMEM) for index, value in enumerate(operands)]
    return pl.pallas_call(
        kernel,
        out_shape=outputs,
        in_specs=[specs.get(index, VMEM) for index in range(len(operands))],
        out_specs=settings.pop("out_specs", jax.tree.map(lambda _: VMEM, outputs)),
        scratch_shapes=list(scratch),
        compiler_params=pltpu.CompilerParams(vmem_limit_bytes=KERNEL_BYTES),
        **settings,
    )(*operands)


def spread(row_value, band_value, shape, carried):
    row_held, band_held, row_late, band_late = row_value, band_value, None, None
    for row_pairs, band_pairs in zip(row_rounds(shape, carried), band_rounds(shape, carried)):
        if row_late is not None:
            row_held, band_held = row_held + row_late, band_held + band_late
        band_late = send(band_held, band_pairs)
        row_late = send(row_held, row_pairs)
    band_held = band_held + band_late
    lanes = shape[0] // shape[1]
    return [row_held, row_late, band_held] + [within_group(band_held, shape, shift) for shift in range(1, lanes)]


def finish(pieces, width, tall, wide):
    last_stay, others, last_in, others_in, col_in, corner_in = pieces
    result = jax.ShapeDtypeStruct((tall, wide), F32)
    count = wide // width
    partial = call(
        functools.partial(local_fill_kernel, width),
        result,
        (last_stay, others),
        [pltpu.SemaphoreType.DMA((count,))],
        out_specs=ANY,
    )
    return call(
        functools.partial(fill_kernel, width),
        result,
        (partial, last_in, others_in, col_in, corner_in),
        [pltpu.SemaphoreType.DMA((count + 2,))],
        specs={0: ANY},
        out_specs=ANY,
        input_output_aliases={0: 0},
    )


def shards(shape, matrix, gap_table, orders):
    rows, cols = shape
    band_pairs = rows // cols
    width = gap_table.shape[2]
    steps = orders.shape[0]
    tall, wide = matrix.shape
    square = pltpu.VMEM((width, width), F32)
    many = pltpu.VMEM((width, wide - 2 * width), F32)
    stack = pltpu.VMEM((1 + band_pairs, width, width), F32)
    row_stack, band_stack = (pltpu.VMEM((count, 6, width, width), BF16) for count in (1, band_pairs))
    dma = pltpu.SemaphoreType.DMA

    row_value = call(
        functools.partial(first_generators_kernel, shape),
        square,
        (matrix, gap_table),
        [square, square, dma((2,))],
        specs={0: HBM, 1: HBM},
    )
    band_value = lax.optimization_barrier(row_value)

    last_pair = band_pairs - 1
    for step in range(steps):
        carried = int(step > 0)
        parts = spread(row_value, band_value, shape, carried)
        if step == steps - 1:
            split_factors = call(
                functools.partial(weights_kernel, shape, carried), (row_stack, band_stack), parts, [stack, stack]
            )
        else:
            if step > 0:
                matrix = finish(pieces, width, tall, wide)
            wanted = [
                ((row + 1) % rows * cols + (row + 1) % rows // band_pairs, row * cols + (row + 1) % rows // band_pairs)
                for row in range(rows)
            ]
            next_gap = send(gap_table[step + 1], wanted)
            band_factors = call(
                functools.partial(band_weights_kernel, shape, carried),
                band_stack,
                parts[2:],
                [pltpu.VMEM((band_pairs, width, width), F32)] * 2,
            )
            row_factors, row_value, band_value = call(
                functools.partial(row_weights_and_next_kernel, shape, step),
                (row_stack, square, square),
                (orders, matrix, gap_table, next_gap, band_factors, *parts[:2]),
                [pltpu.VMEM((1, width, width), F32)] * 2,
                specs={0: SMEM},
            )
            split_factors = (row_factors, band_factors)
        if step < steps - 1 or steps == 1:
            tiles = lambda pair: tuple((0, i * width, (2 * pair + j) * width) for i in (0, 1) for j in (0, 1))
            last_inputs, last_tiles = (matrix,), (tiles(last_pair),)
            other_inputs, other_tiles = (matrix,), tuple(tiles(pair) for pair in range(last_pair))
        else:
            last_stay, others, last_in, others_in, col_in, corner_in = pieces
            last_inputs = (last_stay, others, last_in, others_in)
            edge = (2 * last_pair - 1) * width
            last_tiles = (((0, 0, 0), (1, 0, edge), (2, 0, 0), (3, 0, edge)),)
            other_inputs = (others, others_in, col_in, corner_in)
            other_tiles = tuple(
                tuple(
                    (side, 0, 2 * pair * width) if slot == 0 else (side, 0, (2 * pair - 1) * width) if pair else (2 + side, 0, 0)
                    for side in (0, 1)
                    for slot in (0, 1)
                )
                for pair in range(last_pair)
            )
        last_stay, last_leave, col_piece, corner_piece = call(
            functools.partial(rotate_kernel, shape, step, (last_pair,), last_tiles),
            (square,) * 4,
            (orders, *last_inputs, *split_factors),
            specs={0: SMEM},
        )
        others, others_leave = call(
            functools.partial(rotate_kernel, shape, step, tuple(range(last_pair)), other_tiles),
            (many, many),
            (orders, *other_inputs, *split_factors),
            specs={0: SMEM},
        )
        col_in = to_next_cols(col_piece, shape)
        corner_in = to_next_corner(corner_piece, shape)
        last_in = to_next_rows(last_leave, shape)
        others_in = to_next_rows(others_leave, shape)
        pieces = (last_stay, others, last_in, others_in, col_in, corner_in)
    return finish(pieces, width, tall, wide)


def solution(mesh):
    shape = (mesh.shape["rows"], mesh.shape["cols"])
    in_specs = (P("rows", "cols"), P(None, "rows", None), P())
    out_specs = P("rows", "cols")

    def body(matrix, gap_table, orders):
        return shards(shape, matrix, gap_table, orders)

    return jax.shard_map(body, mesh=mesh, in_specs=in_specs, out_specs=out_specs, check_vma=False)
```
